512 devices in a mesh: dp: 128 (over y_lo, z, x), fsdp: 4 (over y_hi, core).
Axes of the slice: x: 4, y: 4 (y_hi: 2, y_lo: 2; y = y_hi * 2 + y_lo), z: 16, core: 2. Of those that a mesh axis runs over, the one named last changes fastest.
Arguments:
- cached: bfloat16 [128, 4, 256, 1024], P('dp', 'fsdp'), may hold values from -60 to 60
- send_rows: int32 [128, 4, 128, 4], P('dp', 'fsdp'), may hold values from -1 to 255, as said below
- take_rows: int32 [128, 4, 256], P('dp', 'fsdp'), may hold values from -1 to 511, as said below
- utt_index: int32 [128, 4, 256], P('dp', 'fsdp'), may hold values from 0 to 9, never falling along the last dimension, each value on 1 to 64 neighbouring positions
- upstream: bfloat16 [128, 4, 512, 1536], P('dp', 'fsdp'), may hold values from -6 to 6
- in_proj: bfloat16 [512, 1536], P(None, 'fsdp'), may hold values from -2 to 2
- norm_gain: bfloat16 [1536], P('fsdp'), may hold values from 0.099609375 to 1.8984375
- conv_kernel: bfloat16 [31, 1536], P(None, 'fsdp'), may hold values from -1 to 1
Outputs:
- grad_proj: float32 [512, 1536], P(None, 'fsdp')
- grad_kernel: float32 [31, 1536], P(None, 'fsdp')
- grad_gain: float32 [1536], P('fsdp')
- step_loss: float32 [128, 4], P('dp', 'fsdp')
The draws below stay inside these ranges and needn't reach their ends.
Inputs may be any that keep to these rules, and one draw needn't show every extreme that they name: `send_rows`: entry [s, g, d, j] is -1 or the cache row of sender s (same fsdp group g) sent as entry j of its slot for device d. The used entries of a slot come first; a sender's used entries for one device lie in one aligned block of 4 cache rows; a sender's entries name distinct rows. Each device receives from 64 senders of its group, and some device of each group receives 4 rows from each of them. `take_rows`: entry [d, g, r] is -1 or s * 4 + j for a used entry send_rows[s, g, d, j]; each used entry is named once. The -1 entries of a device come last, the rows from one sender stand together, and some device of each group has no -1 entry. Sender 128 - 1 fills its whole slot for every device that it serves.
All inputs are finite; a program needn't handle non-finite values.
Results may differ from the reference program's by a relative error of at most 0.003.
Values may be sent and summed in bfloat16 or wider, within the bound.
A program may use at most 64 MiB of HBM per device.

```python
import math
import jax
import jax.numpy as jnp
import numpy as np
from jax import lax

FEAT = 128
STACK = 4
D = 1536
KW = 31
PAIRS = 256
UTT_MOST = 64
SLOT = 4
UTTS = 10
N_DP = 128
N_FSDP = 4


def routing(key):
    senders = N_DP
    owner_count = N_DP // 2

    def one_group(group_key):
        subkeys = jax.random.split(group_key, 6)
        dest_perm = jax.random.permutation(subkeys[0], senders)
        send_perm = jax.random.permutation(subkeys[1], senders)
        offsets = jax.random.permutation(subkeys[2], senders)[:owner_count]
        owners = send_perm[(dest_perm[:, None] + offsets[None, :]) % senders]
        piece_lens = jax.random.randint(subkeys[3], (senders, owner_count), 1, SLOT + 1)
        full_dest = jax.random.randint(subkeys[4], (), 0, senders)
        piece_lens = jnp.where(jnp.arange(senders)[:, None] == full_dest, SLOT, piece_lens)
        piece_lens = jnp.where(owners == senders - 1, SLOT, piece_lens)
        ends = jnp.cumsum(piece_lens, axis=1)
        starts = ends - piece_lens
        live_total = ends[:, -1]
        row_ids = jnp.arange(PAIRS)
        piece_of = jnp.sum((starts[:, None, :] <= row_ids[None, :, None]).astype(jnp.int32), axis=2) - 1
        piece_start = jnp.take_along_axis(starts, piece_of, axis=1)
        piece_owner = jnp.take_along_axis(owners, piece_of, axis=1)
        take_list = jnp.where(row_ids[None, :] < live_total[:, None], piece_owner * SLOT + row_ids[None, :] - piece_start, -1)
        rotation = jax.random.randint(subkeys[5], (senders, owner_count), 0, SLOT)
        slot_ids = jnp.arange(SLOT)
        block_ids = jnp.arange(owner_count)
        cache_ids = block_ids[None, :, None] * SLOT + (slot_ids[None, None, :] + rotation[:, :, None]) % SLOT
        cache_ids = jnp.where(slot_ids[None, None, :] < piece_lens[:, :, None], cache_ids, -1)
        send_list = jnp.full((senders, senders, SLOT), -1, jnp.int32)
        send_list = send_list.at[owners, jnp.arange(senders)[:, None]].set(cache_ids.astype(jnp.int32))
        return (send_list, take_list.astype(jnp.int32))
    group_keys = jax.random.split(key, N_FSDP)
    send_all, take_all = jax.vmap(one_group)(group_keys)
    return (jnp.transpose(send_all, (1, 0, 2, 3)).astype(jnp.int32), jnp.transpose(take_all, (1, 0, 2)).astype(jnp.int32))


def draw_send_rows(key, part):
    return routing(jax.random.fold_in(key, 11))[0]


def draw_take_rows(key, part):
    return routing(jax.random.fold_in(key, 11))[1]


def draw_cached(key, part):
    subkeys = jax.random.split(jax.random.fold_in(key, 23), 3)
    shape = (N_DP, N_FSDP, PAIRS, 2 * STACK, FEAT)
    base = jnp.clip(jax.random.normal(subkeys[0], shape, jnp.float32), -5.0, 5.0)
    frame_scale = jnp.exp(jax.random.uniform(subkeys[1], (N_DP, N_FSDP, PAIRS, 2 * STACK, 1), jnp.float32, -1.15, 1.15))
    feat_scale = jnp.exp(jax.random.uniform(subkeys[2], (FEAT,), jnp.float32, -1.15, 1.15))
    values_all = base * frame_scale * feat_scale
    return values_all.reshape(N_DP, N_FSDP, PAIRS, 2 * STACK * FEAT).astype(jnp.bfloat16)


def draw_in_proj(key, part):
    subkeys = jax.random.split(jax.random.fold_in(key, 37), 2)
    shape = (STACK * FEAT, D)
    column_scale = jnp.exp(jax.random.uniform(subkeys[1], (D,), jnp.float32, -1.15, 1.15))
    base = jnp.clip(jax.random.normal(subkeys[0], shape, jnp.float32), -4.0, 4.0)
    return (base * column_scale / math.sqrt(STACK * FEAT)).astype(jnp.bfloat16)


def block_levels(key, dims, cuts, least, largest):
    def one(position, parts):
        steps = jax.random.uniform(jax.random.fold_in(jax.random.fold_in(key, 6), position), (parts,), jnp.float32, least / len(cuts), largest / len(cuts))
        return jnp.repeat(jnp.exp(steps), dims[position] // parts).reshape((-1,) + (1,) * (len(dims) - position - 1))

    factor_of = one(*cuts[0])
    for cut in cuts[1:]:
        factor_of = factor_of * one(*cut)
    return factor_of


def split_up(count, total, reach, lean):
    portions = [(1 << 20) // math.isqrt(grade ** lean) + 1 for grade in range(2, count + 1)]
    rest, holding = total - reach - (count - 1), [1] * (count - 1)
    while rest > 0:
        candidates = [i for i in range(count - 1) if holding[i] < reach]
        pool, left = sum([portions[i] for i in candidates]), rest
        for i in candidates:
            addition = min(reach - holding[i], max(1, left * portions[i] // pool), rest)
            holding[i] = holding[i] + addition
            rest = rest - addition
    return np.array([reach] + holding)


def uneven_parts(own_key, count, total, bound, slope):
    if count == 2:
        one = jax.random.randint(own_key, (), max(1, total - bound), min(bound, total - 1) + 1)
        return jnp.stack([one, total - one])
    tallies = jnp.asarray(split_up(count, total, bound, slope), jnp.int32)
    twos = (count - 1) // 2
    source_of, receiver = tallies[1:1 + 2 * twos:2], tallies[2:2 + 2 * twos:2]
    margin = jnp.minimum(source_of - 1, bound - receiver)
    shifted = jax.random.randint(jax.random.fold_in(own_key, 1), (twos,), 0, 1 << 20) % (margin + 1)
    tallies = tallies.at[1:1 + 2 * twos:2].set(source_of - shifted).at[2:2 + 2 * twos:2].set(receiver + shifted)
    return tallies[jax.random.permutation(jax.random.fold_in(own_key, 2), count)]


def noise(own_key, extent, width, bound, cuts=(), held_as=jnp.bfloat16):
    array = width * jax.random.normal(own_key, extent, jnp.float32)
    if cuts:
        array = array * block_levels(own_key, extent, cuts, -0.22, 0.18)
    return jnp.clip(array, -bound, bound).astype(held_as)


def setup_inputs(seed: int = 0) -> dict:
    seeds = jax.random.split(jax.random.key(seed), 9)
    return {
        "cached": draw_cached(jax.random.fold_in(seeds[8], 71), 0),
        "send_rows": draw_send_rows(jax.random.fold_in(seeds[8], 71), 0),
        "take_rows": draw_take_rows(jax.random.fold_in(seeds[8], 71), 0),
        "utt_index": jax.vmap(lambda own: jnp.searchsorted(jnp.cumsum(uneven_parts(own, UTTS, PAIRS, UTT_MOST, 1)), jnp.arange(PAIRS), side="right"))(jax.random.split(seeds[3], N_DP * N_FSDP)).reshape((N_DP, N_FSDP, PAIRS)).astype(jnp.int32),
        "upstream": noise(seeds[4], (N_DP, N_FSDP, 2 * PAIRS, D), 1.0, 6.0, ((0, 128), (1, 4))),
        "in_proj": draw_in_proj(jax.random.fold_in(seeds[8], 71), 0),
        "norm_gain": jnp.clip(1.0 + 0.18 * jax.random.normal(seeds[6], (D,), jnp.float32), 0.099609375, 1.8984375).astype(jnp.bfloat16),
        "conv_kernel": noise(seeds[7], (KW, D), KW ** -0.5, 1.0, ((1, 4),)),
    }


def spread_conv(source_field, kernel_taps, tap_weights):
    tap_count = kernel_taps.shape[0]
    half_width = tap_count // 2
    step_count = source_field.shape[0]
    padded = jnp.pad(source_field, ((half_width, half_width), (0, 0)))
    summed = jnp.zeros_like(source_field)
    for offset in range(tap_count):
        summed = summed + kernel_taps[offset] * (tap_weights[:, offset:offset + 1] * padded[offset:offset + step_count])
    return summed

def build_mask(live_steps, utterances, tap_count):
    half_width = tap_count // 2
    step_count = live_steps.shape[0]
    live_pad = jnp.pad(live_steps, (half_width, half_width))
    utter_pad = jnp.pad(utterances, (half_width, half_width), constant_values=-1)
    columns = []
    for offset in range(tap_count):
        columns.append(live_steps & live_pad[offset:offset + step_count] & (utterances == utter_pad[offset:offset + step_count]))
    return jnp.stack(columns, axis=1).astype(jnp.float32)

def layer_terms(encoded, live_steps, utterances, grad_above, gain, kernel):
    tap_count = kernel.shape[0]
    half_width = tap_count // 2
    step_count = encoded.shape[0]
    tap_weights = build_mask(live_steps, utterances, tap_count)
    row_mean = lax.optimization_barrier(jnp.mean(encoded, axis=1, keepdims=True))
    centered = encoded - row_mean
    row_var = lax.optimization_barrier(jnp.mean(centered * centered, axis=1, keepdims=True))
    inv_std = lax.rsqrt(row_var + 1e-05)
    normalized = centered * inv_std
    gain_f32 = gain.astype(jnp.float32)
    kernel_taps = kernel.astype(jnp.float32)
    normed = normalized * gain_f32
    conv_out = spread_conv(normed, kernel_taps, tap_weights)
    gate_sig = jax.nn.sigmoid(conv_out)
    output = encoded + conv_out * gate_sig
    scale = (encoded.shape[0] * encoded.shape[1]) ** (-0.5)
    grad_out = jnp.where(live_steps[:, None], grad_above.astype(jnp.float32), jnp.zeros((), jnp.float32)) * scale
    device_loss = jnp.sum(output * grad_out)
    grad_conv = grad_out * (gate_sig * (1.0 + conv_out * (1.0 - gate_sig)))
    grad_normed = spread_conv(grad_conv, kernel_taps[::-1], tap_weights)
    padded = jnp.pad(normed, ((half_width, half_width), (0, 0)))
    grad_taps = jnp.stack([lax.optimization_barrier(jnp.sum(grad_conv * tap_weights[:, offset:offset + 1] * padded[offset:offset + step_count], axis=0)) for offset in range(tap_count)])
    grad_scale = lax.optimization_barrier(jnp.sum(grad_normed * normalized, axis=0))
    grad_hat = grad_normed * gain_f32
    grad_x = grad_out + inv_std * (grad_hat - lax.optimization_barrier(jnp.mean(grad_hat, axis=1, keepdims=True)) - normalized * lax.optimization_barrier(jnp.mean(grad_hat * normalized, axis=1, keepdims=True)))
    return (device_loss, grad_x.astype(jnp.bfloat16), grad_taps, grad_scale)

def reference(cached, send_rows, take_rows, utt_index, upstream, in_proj, norm_gain, conv_kernel):
    is_live = take_rows >= 0
    safe_index = jnp.maximum(take_rows, 0).astype(jnp.int32)
    sender = (safe_index // SLOT).astype(jnp.int32)
    slot_entry = (safe_index % SLOT).astype(jnp.int32)
    fsdp_index = jnp.arange(N_FSDP).astype(jnp.int32)[None, :, None]
    destination = jnp.arange(N_DP).astype(jnp.int32)[:, None, None]
    cache_index = jnp.maximum(send_rows[sender, fsdp_index, destination, slot_entry], 0).astype(jnp.int32)
    work_rows = cached[sender, fsdp_index, cache_index]
    work_rows = jnp.where(is_live[..., None], work_rows, jnp.zeros((), cached.dtype))
    devices_all = N_DP * N_FSDP
    work_flat = work_rows.reshape(devices_all, PAIRS, 2 * STACK * FEAT)
    live_flat = is_live.reshape(devices_all, PAIRS)
    utter_flat = utt_index.reshape(devices_all, PAIRS)
    above_flat = upstream.reshape(devices_all, 2 * PAIRS, D)
    proj_f32 = in_proj.astype(jnp.float32)

    def device_step(running, inputs):
        pair_rows, live_pairs, utter_pairs, grad_above = inputs
        frames = pair_rows.reshape(2 * PAIRS, STACK * FEAT).astype(jnp.float32)
        live_steps = jnp.repeat(live_pairs, 2)
        utterances = jnp.repeat(utter_pairs, 2)
        encoded = jnp.dot(frames, proj_f32, precision=lax.Precision.HIGHEST)
        device_loss, grad_x, grad_taps, grad_scale = layer_terms(encoded, live_steps, utterances, grad_above, norm_gain, conv_kernel)
        grad_weight = jnp.dot(frames.T, grad_x.astype(jnp.float32), precision=lax.Precision.HIGHEST)
        return ((running[0] + grad_weight, running[1] + grad_taps, running[2] + grad_scale), device_loss)
    initial = (jnp.zeros((STACK * FEAT, D), jnp.float32), jnp.zeros((KW, D), jnp.float32), jnp.zeros((D,), jnp.float32))
    totals, losses = lax.scan(device_step, initial, (work_flat, live_flat, utter_flat, above_flat))
    return (totals[0], totals[1], totals[2], losses.reshape(N_DP, N_FSDP))
```

```python
import functools

import jax
import jax.numpy as jnp
from jax import lax
from jax.experimental import pallas as pl
from jax.experimental.pallas import tpu as pltpu
from jax.sharding import PartitionSpec as P

LANES = 128
RING = 4
Z_SIZE = 16
UNIT = 16
Z_OWNERS = 13
X_ROWS = Z_OWNERS * UNIT
Y_ROWS = RING * X_ROWS
Q_ROWS = 2 * Y_ROWS
MESH_ID = pl.DeviceIdType.MESH


def spread_conv(source_field, kernel_taps, tap_weights):
    tap_count = kernel_taps.shape[0]
    half_width = tap_count // 2
    step_count = source_field.shape[0]
    padded = jnp.pad(source_field, ((half_width, half_width), (0, 0)))
    summed = jnp.zeros_like(source_field)
    for offset in range(tap_count):
        summed = summed + kernel_taps[offset] * (
            tap_weights[:, offset : offset + 1] * padded[offset : offset + step_count]
        )
    return summed


def build_mask(live_steps, utterances, tap_count):
    half_width = tap_count // 2
    step_count = live_steps.shape[0]
    live_pad = jnp.pad(live_steps, (half_width, half_width))
    utter_pad = jnp.pad(utterances, (half_width, half_width), constant_values=-1)
    columns = []
    for offset in range(tap_count):
        columns.append(
            live_steps
            & live_pad[offset : offset + step_count]
            & (utterances == utter_pad[offset : offset + step_count])
        )
    return jnp.stack(columns, axis=1).astype(jnp.float32)


def layer_terms(encoded, live_steps, utterances, grad_above, gain, kernel):
    tap_count = kernel.shape[0]
    half_width = tap_count // 2
    step_count = encoded.shape[0]
    tap_weights = build_mask(live_steps, utterances, tap_count)
    row_mean = jnp.mean(encoded, axis=1, keepdims=True)
    centered = encoded - row_mean
    row_var = jnp.mean(centered * centered, axis=1, keepdims=True)
    inv_std = lax.rsqrt(row_var + 1e-05)
    normalized = centered * inv_std
    gain_f32 = gain.astype(jnp.float32)
    kernel_taps = kernel.astype(jnp.float32)
    normed = normalized * gain_f32
    conv_out = spread_conv(normed, kernel_taps, tap_weights)
    gate_sig = jax.nn.sigmoid(conv_out)
    output = encoded + conv_out * gate_sig
    scale = (encoded.shape[0] * encoded.shape[1]) ** (-0.5)
    grad_out = (
        jnp.where(live_steps[:, None], grad_above.astype(jnp.float32), jnp.zeros((), jnp.float32))
        * scale
    )
    device_loss = jnp.sum(output * grad_out)
    grad_conv = grad_out * (gate_sig * (1.0 + conv_out * (1.0 - gate_sig)))
    grad_normed = spread_conv(grad_conv, kernel_taps[::-1], tap_weights)
    padded = jnp.pad(normed, ((half_width, half_width), (0, 0)))
    grad_taps = jnp.stack(
        [
            jnp.sum(
                grad_conv
                * tap_weights[:, offset : offset + 1]
                * padded[offset : offset + step_count],
                axis=0,
            )
            for offset in range(tap_count)
        ]
    )
    grad_scale = jnp.sum(grad_normed * normalized, axis=0)
    grad_hat = grad_normed * gain_f32
    grad_x = grad_out + inv_std * (
        grad_hat
        - jnp.mean(grad_hat, axis=1, keepdims=True)
        - normalized * jnp.mean(grad_hat * normalized, axis=1, keepdims=True)
    )
    return (device_loss, grad_x.astype(jnp.bfloat16), grad_taps, grad_scale)


def reduce_kernel(
    g_ref, o_ref,
    cbuf, ysend, ystage, yfirst, yfrom,
    xbuf, xstage, xfirst, xfrom,
    zbuf, zfrom, final,
    core_s, core_r, y_s, y_r, x_s, x_r, z_s, z_r, za_s, za_r, xa_s, xa_r, ya_s, ya_r,
):
    p = lax.axis_index("dp")
    f = lax.axis_index("fsdp")
    x = lax.rem(p, RING)
    z = lax.rem(lax.div(p, RING), Z_SIZE)
    y_lo = lax.div(p, RING * Z_SIZE)
    y_hi = lax.div(f, 2)
    core = lax.rem(f, 2)
    y = y_hi * 2 + y_lo

    def at(yy, zz, xx, cc):
        return (
            (lax.rem(yy, 2) * Z_SIZE + zz) * RING + xx,
            lax.div(yy, 2) * 2 + cc,
        )

    y_r1, y_l1, y_op = lax.rem(y + 1, RING), lax.rem(y + 3, RING), lax.rem(y + 2, RING)
    x_r1, x_l1, x_op = lax.rem(x + 1, RING), lax.rem(x + 3, RING), lax.rem(x + 2, RING)
    y_mate = y_hi * 2 + 1 - y_lo
    dev_core = at(y, z, x, 1 - core)
    dev_yr, dev_yl = at(y_r1, z, x, core), at(y_l1, z, x, core)
    dev_xr, dev_xl = at(y, z, x_r1, core), at(y, z, x_l1, core)
    dev_mate = at(y_mate, z, x, core)

    def dev_z(o):
        return at(y, lax.rem(z + o, Z_SIZE), x, core)

    barrier = pltpu.get_barrier_semaphore()
    for d in [dev_core, dev_yr, dev_yl, dev_xr, dev_xl]:
        pl.semaphore_signal(barrier, inc=1, device_id=d, device_id_type=MESH_ID)
    for o in range(1, Z_SIZE):
        pl.semaphore_signal(barrier, inc=1, device_id=dev_z(o), device_id_type=MESH_ID)
    pl.semaphore_wait(barrier, 5 + Z_SIZE - 1)

    def send(src, dst, ssem, rsem, d):
        copy = pltpu.make_async_remote_copy(
            src_ref=src, dst_ref=dst, send_sem=ssem, recv_sem=rsem,
            device_id=d, device_id_type=MESH_ID,
        )
        copy.start()
        return copy

    def piece(yy, cc):
        row = (lax.div(yy, 2) * 2 + cc) * Q_ROWS + lax.rem(yy, 2) * Y_ROWS
        return pl.ds(pl.multiple_of(row, UNIT), Y_ROWS)

    core_copies = []
    for o in (2, 1, 3, 0):
        yy = lax.rem(y + o, RING)
        core_copies.append(
            send(g_ref.at[piece(yy, 1 - core)], cbuf.at[o], core_s.at[o], core_r.at[o], dev_core)
        )
    half = Y_ROWS // 2
    lo, hi = pl.ds(0, half), pl.ds(half, half)

    def summed(o):
        return g_ref[piece(lax.rem(y + o, RING), core)] + cbuf[o]

    core_copies[0].wait_recv()
    ysend[1] = summed(2).astype(jnp.bfloat16)
    y0 = send(ysend.at[1, lo], yfirst.at[0], y_s.at[0], y_r.at[0], dev_yr)
    y1 = send(ysend.at[1, hi], yfirst.at[1], y_s.at[1], y_r.at[1], dev_yl)
    core_copies[1].wait_recv()
    ysend[0] = summed(1).astype(jnp.bfloat16)
    y2 = send(ysend.at[0, hi], yfrom.at[0, hi], y_s.at[2], y_r.at[2], dev_yr)
    core_copies[2].wait_recv()
    ysend[2] = summed(3).astype(jnp.bfloat16)
    y3 = send(ysend.at[2, lo], yfrom.at[1, lo], y_s.at[3], y_r.at[3], dev_yl)
    core_copies[3].wait_recv()
    y0.wait_recv()
    part = g_ref[piece(y_r1, core)] + cbuf[1]
    ystage[0] = (part[:half] + yfirst[0].astype(jnp.float32)).astype(jnp.bfloat16)
    y4 = send(ystage.at[0], yfrom.at[0, lo], y_s.at[4], y_r.at[4], dev_yr)
    y1.wait_recv()
    part = g_ref[piece(y_l1, core)] + cbuf[3]
    ystage[1] = (part[half:] + yfirst[1].astype(jnp.float32)).astype(jnp.bfloat16)
    y5 = send(ystage.at[1], yfrom.at[1, hi], y_s.at[5], y_r.at[5], dev_yl)
    for copy in (y2, y3, y4, y5):
        copy.wait_recv()
    xbuf[...] = (
        summed(0) + yfrom[0].astype(jnp.float32) + yfrom[1].astype(jnp.float32)
    ).reshape(RING, X_ROWS, LANES)

    xh = X_ROWS // 2
    xlo, xhi = pl.ds(0, xh), pl.ds(xh, xh)
    x0 = send(xbuf.at[x_op, xlo], xfirst.at[0], x_s.at[0], x_r.at[0], dev_xr)
    x1 = send(xbuf.at[x_op, xhi], xfirst.at[1], x_s.at[1], x_r.at[1], dev_xl)
    x2 = send(xbuf.at[x_r1, xhi], xfrom.at[0, xhi], x_s.at[2], x_r.at[2], dev_xr)
    x3 = send(xbuf.at[x_l1, xlo], xfrom.at[1, xlo], x_s.at[3], x_r.at[3], dev_xl)
    x0.wait_recv()
    xstage[0] = xbuf[x_r1, xlo] + xfirst[0]
    x4 = send(xstage.at[0], xfrom.at[0, xlo], x_s.at[4], x_r.at[4], dev_xr)
    x1.wait_recv()
    xstage[1] = xbuf[x_l1, xhi] + xfirst[1]
    x5 = send(xstage.at[1], xfrom.at[1, xhi], x_s.at[5], x_r.at[5], dev_xl)
    for copy in (x2, x3, x4, x5):
        copy.wait_recv()
    zbuf[...] = (xbuf[x] + xfrom[0] + xfrom[1]).reshape(Z_OWNERS, UNIT, LANES)

    def z_copy(o):
        to = lax.rem(z + o, Z_SIZE)
        return pltpu.make_async_remote_copy(
            src_ref=zbuf.at[lax.min(to, Z_OWNERS - 1)],
            dst_ref=zfrom.at[o - 1],
            send_sem=z_s.at[o - 1],
            recv_sem=z_r.at[o - 1],
            device_id=dev_z(o),
            device_id_type=MESH_ID,
        )

    def own_rows(zz):
        row = y_lo * Y_ROWS + x * X_ROWS + lax.min(zz, Z_OWNERS - 1) * UNIT
        return final.at[pl.ds(pl.multiple_of(row, UNIT), UNIT)]

    def za_copy(o, zz):
        return pltpu.make_async_remote_copy(
            src_ref=own_rows(zz),
            dst_ref=own_rows(zz),
            send_sem=za_s.at[o - 1],
            recv_sem=za_r.at[o - 1],
            device_id=dev_z(o),
            device_id_type=MESH_ID,
        )

    for o in range(1, Z_SIZE):
        @pl.when(lax.rem(z + o, Z_SIZE) < Z_OWNERS)
        def _():
            z_copy(o).start()

    @pl.when(z < Z_OWNERS)
    def _():
        total = zbuf[lax.min(z, Z_OWNERS - 1)]
        for o in range(1, Z_SIZE):
            z_copy(o).wait_recv()
            total = total + zfrom[o - 1]
        row = y_lo * Y_ROWS + x * X_ROWS + lax.min(z, Z_OWNERS - 1) * UNIT
        final[pl.ds(pl.multiple_of(row, UNIT), UNIT)] = total.astype(jnp.bfloat16)
        for o in range(1, Z_SIZE):
            za_copy(o, z).start()

    for o in range(1, Z_SIZE):
        source = lax.rem(z + Z_SIZE - o, Z_SIZE)
        @pl.when(source < Z_OWNERS)
        def _():
            za_copy(o, source).wait_recv()

    def rows(xx, start, size):
        row = y_lo * Y_ROWS + xx * X_ROWS + start
        return final.at[pl.ds(pl.multiple_of(row, UNIT), size)]

    cut = 7 * UNIT
    mine = rows(x, 0, X_ROWS)
    a0 = send(mine, mine, xa_s.at[0], xa_r.at[0], dev_xr)
    a1 = send(mine, mine, xa_s.at[1], xa_r.at[1], dev_xl)
    b0 = send(mine, mine, ya_s.at[0], ya_r.at[0], dev_mate)
    a0.wait_recv()
    ring_lo = rows(x_l1, 0, cut)
    a2 = send(ring_lo, ring_lo, xa_s.at[2], xa_r.at[2], dev_xr)
    got = rows(x_l1, 0, X_ROWS)
    b1 = send(got, got, ya_s.at[1], ya_r.at[1], dev_mate)
    a1.wait_recv()
    ring_hi = rows(x_r1, cut, X_ROWS - cut)
    a3 = send(ring_hi, ring_hi, xa_s.at[3], xa_r.at[3], dev_xl)
    got = rows(x_r1, 0, X_ROWS)
    b2 = send(got, got, ya_s.at[2], ya_r.at[2], dev_mate)
    a2.wait_recv()
    a3.wait_recv()
    got = rows(x_op, 0, X_ROWS)
    b3 = send(got, got, ya_s.at[3], ya_r.at[3], dev_mate)
    for copy in (b0, b1, b2, b3):
        copy.wait_recv()

    tile_rows = o_ref.shape[0]
    for i in range(o_ref.shape[1] // LANES):
        o_ref[:, i * LANES : (i + 1) * LANES] = final[
            i * tile_rows : (i + 1) * tile_rows
        ].astype(jnp.float32)

    for copy in core_copies + [y0, y1, y2, y3, y4, y5, x0, x1, x2, x3, x4, x5]:
        copy.wait_send()
    for o in range(1, Z_SIZE):
        @pl.when(lax.rem(z + o, Z_SIZE) < Z_OWNERS)
        def _():
            z_copy(o).wait_send()

    @pl.when(z < Z_OWNERS)
    def _():
        for o in range(1, Z_SIZE):
            za_copy(o, z).wait_send()
    for copy in (a0, a1, a2, a3, b0, b1, b2, b3):
        copy.wait_send()


def reduce_gradients(packed, rows, cols):
    f32, bf16 = jnp.float32, jnp.bfloat16
    half, xh = Y_ROWS // 2, X_ROWS // 2
    dma = pltpu.SemaphoreType.DMA
    return pl.pallas_call(
        reduce_kernel,
        out_shape=jax.ShapeDtypeStruct((rows, cols), f32),
        in_specs=[pl.BlockSpec(memory_space=pltpu.VMEM)],
        out_specs=pl.BlockSpec(memory_space=pltpu.VMEM),
        scratch_shapes=[
            pltpu.VMEM((RING, Y_ROWS, LANES), f32),
            pltpu.VMEM((3, Y_ROWS, LANES), bf16),
            pltpu.VMEM((2, half, LANES), bf16),
            pltpu.VMEM((2, half, LANES), bf16),
            pltpu.VMEM((2, Y_ROWS, LANES), bf16),
            pltpu.VMEM((RING, X_ROWS, LANES), f32),
            pltpu.VMEM((2, xh, LANES), f32),
            pltpu.VMEM((2, xh, LANES), f32),
            pltpu.VMEM((2, X_ROWS, LANES), f32),
            pltpu.VMEM((Z_OWNERS, UNIT, LANES), f32),
            pltpu.VMEM((Z_SIZE - 1, UNIT, LANES), f32),
            pltpu.VMEM((Q_ROWS, LANES), bf16),
            dma((RING,)), dma((RING,)),
            dma((6,)), dma((6,)),
            dma((6,)), dma((6,)),
            dma((Z_SIZE - 1,)), dma((Z_SIZE - 1,)),
            dma((Z_SIZE - 1,)), dma((Z_SIZE - 1,)),
            dma((4,)), dma((4,)),
            dma((4,)), dma((4,)),
        ],
        compiler_params=pltpu.CompilerParams(
            collective_id=0, has_side_effects=True, vmem_limit_bytes=40 << 20
        ),
        name="reduce_gradients",
    )(packed)


def per_device(cached, send_rows, take_rows, utt_index, upstream, in_proj, norm_gain, conv_kernel):
    cache_rows = cached[0, 0]
    wanted = send_rows[0, 0]
    outgoing = cache_rows[jnp.maximum(wanted, 0)]
    proj_full, taps_full, gain_full = (
        lax.all_gather(in_proj, "fsdp", axis=1, tiled=True),
        lax.all_gather(conv_kernel, "fsdp", axis=1, tiled=True),
        lax.all_gather(norm_gain[None, :], "fsdp", axis=1, tiled=True),
    )
    take_list = take_rows[0, 0]
    is_live = take_list >= 0
    safe_index = jnp.maximum(take_list, 0)
    pair_count = take_list.shape[0]
    step_width = cache_rows.shape[1] // 2
    arrived = lax.all_to_all(outgoing, "dp", split_axis=0, concat_axis=0, tiled=True)
    flat_rows = arrived.reshape(-1, arrived.shape[2])
    work_rows = jnp.where(is_live[:, None], flat_rows[safe_index], jnp.zeros((), flat_rows.dtype))
    frames = work_rows.reshape(2 * pair_count, step_width)
    encoded = jnp.dot(frames, proj_full, preferred_element_type=jnp.float32)
    live_steps = jnp.repeat(is_live, 2)
    utterances = jnp.repeat(utt_index[0, 0], 2)
    device_loss, grad_x, grad_taps, grad_scale = layer_terms(
        encoded, live_steps, utterances, upstream[0, 0], gain_full[0], taps_full
    )
    grad_weight = lax.dot_general(
        frames, grad_x, (((0,), (0,)), ((), ())), preferred_element_type=jnp.float32
    )
    depth, width = grad_weight.shape
    taps = grad_taps.shape[0]
    rows = depth + taps + 1
    quarters = width // in_proj.shape[1]
    stacked = jnp.concatenate([grad_weight, grad_taps, grad_scale[None, :]], axis=0)
    tiles = stacked.reshape(rows, width // LANES, LANES).transpose(1, 0, 2)
    packed = tiles.reshape(quarters, -1, LANES)
    packed = jnp.pad(packed, ((0, 0), (0, Q_ROWS - packed.shape[1]), (0, 0)))
    total = reduce_gradients(packed.reshape(-1, LANES), rows, in_proj.shape[1])
    return (
        total[:depth],
        total[depth : depth + taps],
        total[depth + taps],
        device_loss.reshape(1, 1),
    )


def solution(mesh):
    placed = (
        P("dp", "fsdp", None, None),
        P("dp", "fsdp", None, None),
        P("dp", "fsdp", None),
        P("dp", "fsdp", None),
        P("dp", "fsdp", None, None),
        P(None, "fsdp"),
        P("fsdp"),
        P(None, "fsdp"),
    )
    return jax.shard_map(
        per_device,
        mesh=mesh,
        in_specs=placed,
        out_specs=(P(None, "fsdp"), P(None, "fsdp"), P("fsdp"), P("dp", "fsdp")),
        check_vma=False,
    )
```

```python
import functools

import jax
import jax.numpy as jnp
from jax import lax
from jax.experimental import pallas as pl
from jax.experimental.pallas import tpu as pltpu
from jax.sharding import PartitionSpec as P

LANES = 128
RING = 4
Z_SIZE = 16
UNIT = 16
Z_OWNERS = 13
X_ROWS = Z_OWNERS * UNIT
Y_ROWS = RING * X_ROWS
Q_ROWS = 2 * Y_ROWS
MESH_ID = pl.DeviceIdType.MESH


SUB = 8
SPAN = 42
HALO = 8
TAPS = 31
REACH = TAPS // 2
BLOCK = 7
GAP = 8
ROWS = SPAN * SUB


def module_kernel(fr_ref, up_ref, w_ref, gain_ref, taps_ref, out_ref, loss_ref,
                  x_s, xh_s, go_s, h_s, inv_s, gc_s, sh_s, shx_s, gx_s, ft_s):
    f32, bf16 = jnp.float32, jnp.bfloat16
    tiles = gain_ref.shape[0]
    width = tiles * LANES
    depth = w_ref.shape[0]
    scale = (2 * 256 * width) ** (-0.5)

    for h in range(2):
        frame = fr_ref[:, h * depth : (h + 1) * depth]
        ft_s[:, h * ROWS : (h + 1) * ROWS] = frame.T
        x_s[h] = jnp.dot(frame, w_ref[...], preferred_element_type=f32)

    def norm_rows(i, loss):
        for h in range(2):
            at = pl.ds(pl.multiple_of(i * 16, 16), 16)
            xv = x_s[h, at, :]
            mean = jnp.sum(xv, axis=1, keepdims=True) * (1.0 / width)
            cen = xv - mean
            var = jnp.sum(cen * cen, axis=1, keepdims=True) * (1.0 / width)
            inv = lax.rsqrt(var + 1e-05)
            inv_s[h, pl.ds(2 * i, 2)] = jnp.broadcast_to(inv, (16, LANES)).reshape(2, SUB, LANES)
            for c in range(tiles):
                lanes = slice(c * LANES, (c + 1) * LANES)
                up = up_ref[pl.ds(pl.multiple_of(h * ROWS + i * 16, 16), 16), lanes]
                go = up.astype(f32) * scale
                go_s[c, h, pl.ds(2 * i, 2)] = go.reshape(2, SUB, LANES)
                xh_s[c, h, pl.ds(HALO + 2 * i, 2)] = (cen[:, lanes] * inv).reshape(2, SUB, LANES)
                loss = loss + go * xv[:, lanes]
        return loss

    loss = lax.fori_loop(0, SPAN // 2, norm_rows, jnp.zeros((16, LANES), f32))
    loss = loss[:SUB] + loss[SUB:]

    sub = lax.broadcasted_iota(jnp.int32, (SUB, LANES), 0)

    def fill_halo(ref):
        for h in range(2):
            for j in range(HALO):
                before = pltpu.roll(ref[h, SPAN + j], 1, 0)
                ref[h, j] = jnp.where(sub == 0, 0.0, before)
                after = pltpu.roll(ref[h, HALO + j], SUB - 1, 0)
                ref[h, HALO + SPAN + j] = jnp.where(sub == SUB - 1, 0.0, after)

    spots = [(h, j) for j in range(BLOCK) for h in range(2)]

    def reach_of(h_in, m):
        found = []
        for h, j in spots:
            d = 2 * (m - j) + h_in - h
            if -REACH <= d <= REACH:
                found.append(((h, j), d + REACH))
        return found

    def conv_block(ref, taps, j0):
        accs = {}
        for m in range(-HALO, BLOCK + HALO):
            for h_in in range(2):
                uses = reach_of(h_in, m)
                if not uses:
                    continue
                v = ref[h_in, j0 + (HALO + m)]
                for spot, k in uses:
                    term = taps[k] * v
                    accs[spot] = accs[spot] + term if spot in accs else term
        return accs

    sh_s[...] = jnp.zeros_like(sh_s)
    shx_s[...] = jnp.zeros_like(shx_s)

    def channel_tile(ct, loss):
        xh = xh_s.at[ct]
        fill_halo(xh)
        gain = jnp.broadcast_to(gain_ref[ct], (SUB, LANES))

        def tap(k):
            return jnp.broadcast_to(taps_ref[ct, k : k + 1, :], (SUB, LANES))

        def forward(b, loss):
            j0 = b * BLOCK
            taps = [tap(k) * gain for k in range(TAPS)]
            accs = conv_block(xh, taps, j0)
            for (h, j), c in accs.items():
                sig = 1.0 / (1.0 + jnp.exp(-c))
                go = go_s[ct, h, j0 + j]
                gos = go * sig
                loss = loss + c * gos
                gc_s[h, j0 + (HALO + j)] = gos * (1.0 + c * (1.0 - sig))
            return loss

        loss = lax.fori_loop(0, SPAN // BLOCK, forward, loss)
        fill_halo(gc_s)

        def backward(b, gg):
            j0 = b * BLOCK
            taps = [tap(TAPS - 1 - k) for k in range(TAPS)]
            accs = conv_block(gc_s, taps, j0)
            for (h, j), gn in accs.items():
                v = xh[h, j0 + (HALO + j)]
                gg = gg + gn * v
                hv = gn * gain
                h_s[ct, h, j0 + j] = hv
                sh_s[h, j0 + j] = sh_s[h, j0 + j] + hv
                shx_s[h, j0 + j] = shx_s[h, j0 + j] + hv * v
            return gg

        zero = jnp.zeros((SUB, LANES), f32)
        gg = lax.fori_loop(0, SPAN // BLOCK, backward, zero)

        def tap_sums(b, sums):
            j0 = b * BLOCK
            sums = list(sums)
            gcs = {(h, j): gc_s[h, j0 + (HALO + j)] for h, j in spots}
            for m in range(-HALO, BLOCK + HALO):
                for h_in in range(2):
                    uses = reach_of(h_in, m)
                    if not uses:
                        continue
                    v = xh[h_in, j0 + (HALO + m)]
                    for spot, k in uses:
                        sums[k] = sums[k] + gcs[spot] * v
            return tuple(sums)

        sums = lax.fori_loop(0, SPAN // BLOCK, tap_sums, (zero,) * TAPS)
        base = lax.div(ct, 3) * Q_ROWS + lax.rem(ct, 3) * (depth + TAPS + 1) + depth
        gain_row = gain_ref[ct]
        tail = [jnp.sum(v, axis=0, keepdims=True) * gain_row for v in sums]
        tail.append(jnp.sum(gg, axis=0, keepdims=True))
        out_ref[pl.ds(pl.multiple_of(base, SUB), TAPS + 1), :] = jnp.concatenate(tail, axis=0)
        return loss

    loss = lax.fori_loop(0, tiles, channel_tile, loss)
    loss_ref[...] = jnp.sum(loss, keepdims=True)

    def grad_rows(i, carry):
        for h in range(2):
            two = pl.ds(2 * i, 2)
            mh = jnp.sum(sh_s[h, two], axis=2, keepdims=True) * (1.0 / width)
            mhx = jnp.sum(shx_s[h, two], axis=2, keepdims=True) * (1.0 / width)
            inv = inv_s[h, two]
            for c in range(tiles):
                xv = xh_s[c, h, pl.ds(HALO + 2 * i, 2)]
                gx = go_s[c, h, two] + inv * (h_s[c, h, two] - mh - xv * mhx)
                gx_s[pl.ds(pl.multiple_of(h * ROWS + i * 16, 16), 16), c * LANES : (c + 1) * LANES] = (
                    gx.reshape(16, LANES).astype(bf16)
                )
        return carry

    lax.fori_loop(0, SPAN // 2, grad_rows, 0)

    per = 2 * LANES
    for c in range(0, tiles, 2):
        gw = jnp.dot(ft_s[...], gx_s[:, c * LANES : c * LANES + per], preferred_element_type=f32)
        for k in range(2):
            base = (c + k) // 3 * Q_ROWS + (c + k) % 3 * (depth + TAPS + 1)
            out_ref[base : base + depth, :] = gw[:, k * LANES : (k + 1) * LANES]
    used = 3 * (depth + TAPS + 1)
    for q in range(tiles // 3):
        out_ref[q * Q_ROWS + used : (q + 1) * Q_ROWS, :] = jnp.zeros((Q_ROWS - used, LANES), f32)


def module_terms(frames, above, proj, gain, taps):
    f32, bf16 = jnp.float32, jnp.bfloat16
    tiles = proj.shape[1] // LANES
    depth = proj.shape[0]
    vm = pl.BlockSpec(memory_space=pltpu.VMEM)
    gain_tiles = gain.astype(f32).reshape(tiles, 1, LANES)
    tap_tiles = taps.astype(f32).reshape(TAPS, tiles, LANES).transpose(1, 0, 2)
    rows = (2, SPAN, SUB, LANES)
    return pl.pallas_call(
        module_kernel,
        out_shape=(
            jax.ShapeDtypeStruct((tiles // 3 * Q_ROWS, LANES), f32),
            jax.ShapeDtypeStruct((1, 1), f32),
        ),
        in_specs=[vm] * 5,
        out_specs=(vm, vm),
        scratch_shapes=[
            pltpu.VMEM((2, ROWS, tiles * LANES), f32),
            pltpu.VMEM((tiles, 2, SPAN + 2 * HALO, SUB, LANES), f32),
            pltpu.VMEM((tiles,) + rows, f32),
            pltpu.VMEM((tiles,) + rows, f32),
            pltpu.VMEM(rows, f32),
            pltpu.VMEM((2, SPAN + 2 * HALO, SUB, LANES), f32),
            pltpu.VMEM(rows, f32),
            pltpu.VMEM(rows, f32),
            pltpu.VMEM((2 * ROWS, tiles * LANES), bf16),
            pltpu.VMEM((depth, 2 * ROWS), bf16),
        ],
        compiler_params=pltpu.CompilerParams(vmem_limit_bytes=56 << 20),
        name="module_terms",
    )(frames, above, proj, gain_tiles, tap_tiles)


def reduce_kernel(
    g_ref, o_ref,
    cbuf, ysend, ystage, yfirst, yfrom,
    xbuf, xstage, xfirst, xfrom,
    zbuf, zfrom, final,
    core_s, core_r, y_s, y_r, x_s, x_r, z_s, z_r, za_s, za_r, xa_s, xa_r, ya_s, ya_r,
):
    p = lax.axis_index("dp")
    f = lax.axis_index("fsdp")
    x = lax.rem(p, RING)
    z = lax.rem(lax.div(p, RING), Z_SIZE)
    y_lo = lax.div(p, RING * Z_SIZE)
    y_hi = lax.div(f, 2)
    core = lax.rem(f, 2)
    y = y_hi * 2 + y_lo

    def at(yy, zz, xx, cc):
        return (
            (lax.rem(yy, 2) * Z_SIZE + zz) * RING + xx,
            lax.div(yy, 2) * 2 + cc,
        )

    y_r1, y_l1, y_op = lax.rem(y + 1, RING), lax.rem(y + 3, RING), lax.rem(y + 2, RING)
    x_r1, x_l1, x_op = lax.rem(x + 1, RING), lax.rem(x + 3, RING), lax.rem(x + 2, RING)
    y_mate = y_hi * 2 + 1 - y_lo
    dev_core = at(y, z, x, 1 - core)
    dev_yr, dev_yl = at(y_r1, z, x, core), at(y_l1, z, x, core)
    dev_xr, dev_xl = at(y, z, x_r1, core), at(y, z, x_l1, core)
    dev_mate = at(y_mate, z, x, core)

    def dev_z(o):
        return at(y, lax.rem(z + o, Z_SIZE), x, core)

    barrier = pltpu.get_barrier_semaphore()
    for d in [dev_core, dev_yr, dev_yl, dev_xr, dev_xl]:
        pl.semaphore_signal(barrier, inc=1, device_id=d, device_id_type=MESH_ID)
    for o in range(1, Z_SIZE):
        pl.semaphore_signal(barrier, inc=1, device_id=dev_z(o), device_id_type=MESH_ID)
    pl.semaphore_wait(barrier, 5 + Z_SIZE - 1)

    def send(src, dst, ssem, rsem, d):
        copy = pltpu.make_async_remote_copy(
            src_ref=src, dst_ref=dst, send_sem=ssem, recv_sem=rsem,
            device_id=d, device_id_type=MESH_ID,
        )
        copy.start()
        return copy

    def piece(yy, cc):
        row = (lax.div(yy, 2) * 2 + cc) * Q_ROWS + lax.rem(yy, 2) * Y_ROWS
        return pl.ds(pl.multiple_of(row, UNIT), Y_ROWS)

    core_copies = []
    for o in (2, 1, 3, 0):
        yy = lax.rem(y + o, RING)
        core_copies.append(
            send(g_ref.at[piece(yy, 1 - core)], cbuf.at[o], core_s.at[o], core_r.at[o], dev_core)
        )
    half = Y_ROWS // 2
    lo, hi = pl.ds(0, half), pl.ds(half, half)

    def summed(o):
        return g_ref[piece(lax.rem(y + o, RING), core)] + cbuf[o]

    core_copies[0].wait_recv()
    ysend[1] = summed(2).astype(jnp.bfloat16)
    y0 = send(ysend.at[1, lo], yfirst.at[0], y_s.at[0], y_r.at[0], dev_yr)
    y1 = send(ysend.at[1, hi], yfirst.at[1], y_s.at[1], y_r.at[1], dev_yl)
    core_copies[1].wait_recv()
    ysend[0] = summed(1).astype(jnp.bfloat16)
    y2 = send(ysend.at[0, hi], yfrom.at[0, hi], y_s.at[2], y_r.at[2], dev_yr)
    core_copies[2].wait_recv()
    ysend[2] = summed(3).astype(jnp.bfloat16)
    y3 = send(ysend.at[2, lo], yfrom.at[1, lo], y_s.at[3], y_r.at[3], dev_yl)
    core_copies[3].wait_recv()
    y0.wait_recv()
    part = g_ref[piece(y_r1, core)] + cbuf[1]
    ystage[0] = (part[:half] + yfirst[0].astype(jnp.float32)).astype(jnp.bfloat16)
    y4 = send(ystage.at[0], yfrom.at[0, lo], y_s.at[4], y_r.at[4], dev_yr)
    y1.wait_recv()
    part = g_ref[piece(y_l1, core)] + cbuf[3]
    ystage[1] = (part[half:] + yfirst[1].astype(jnp.float32)).astype(jnp.bfloat16)
    y5 = send(ystage.at[1], yfrom.at[1, hi], y_s.at[5], y_r.at[5], dev_yl)
    for copy in (y2, y3, y4, y5):
        copy.wait_recv()
    xbuf[...] = (
        summed(0) + yfrom[0].astype(jnp.float32) + yfrom[1].astype(jnp.float32)
    ).reshape(RING, X_ROWS, LANES)

    xh = X_ROWS // 2
    xlo, xhi = pl.ds(0, xh), pl.ds(xh, xh)
    x0 = send(xbuf.at[x_op, xlo], xfirst.at[0], x_s.at[0], x_r.at[0], dev_xr)
    x1 = send(xbuf.at[x_op, xhi], xfirst.at[1], x_s.at[1], x_r.at[1], dev_xl)
    x2 = send(xbuf.at[x_r1, xhi], xfrom.at[0, xhi], x_s.at[2], x_r.at[2], dev_xr)
    x3 = send(xbuf.at[x_l1, xlo], xfrom.at[1, xlo], x_s.at[3], x_r.at[3], dev_xl)
    x0.wait_recv()
    xstage[0] = xbuf[x_r1, xlo] + xfirst[0]
    x4 = send(xstage.at[0], xfrom.at[0, xlo], x_s.at[4], x_r.at[4], dev_xr)
    x1.wait_recv()
    xstage[1] = xbuf[x_l1, xhi] + xfirst[1]
    x5 = send(xstage.at[1], xfrom.at[1, xhi], x_s.at[5], x_r.at[5], dev_xl)
    for copy in (x2, x3, x4, x5):
        copy.wait_recv()
    zbuf[...] = (xbuf[x] + xfrom[0] + xfrom[1]).reshape(Z_OWNERS, UNIT, LANES)

    def z_copy(o):
        to = lax.rem(z + o, Z_SIZE)
        return pltpu.make_async_remote_copy(
            src_ref=zbuf.at[lax.min(to, Z_OWNERS - 1)],
            dst_ref=zfrom.at[o - 1],
            send_sem=z_s.at[o - 1],
            recv_sem=z_r.at[o - 1],
            device_id=dev_z(o),
            device_id_type=MESH_ID,
        )

    def own_rows(zz):
        row = y_lo * Y_ROWS + x * X_ROWS + lax.min(zz, Z_OWNERS - 1) * UNIT
        return final.at[pl.ds(pl.multiple_of(row, UNIT), UNIT)]

    def za_copy(o, zz):
        return pltpu.make_async_remote_copy(
            src_ref=own_rows(zz),
            dst_ref=own_rows(zz),
            send_sem=za_s.at[o - 1],
            recv_sem=za_r.at[o - 1],
            device_id=dev_z(o),
            device_id_type=MESH_ID,
        )

    for o in range(1, Z_SIZE):
        @pl.when(lax.rem(z + o, Z_SIZE) < Z_OWNERS)
        def _():
            z_copy(o).start()

    @pl.when(z < Z_OWNERS)
    def _():
        total = zbuf[lax.min(z, Z_OWNERS - 1)]
        for o in range(1, Z_SIZE):
            z_copy(o).wait_recv()
            total = total + zfrom[o - 1]
        row = y_lo * Y_ROWS + x * X_ROWS + lax.min(z, Z_OWNERS - 1) * UNIT
        final[pl.ds(pl.multiple_of(row, UNIT), UNIT)] = total.astype(jnp.bfloat16)
        for o in range(1, Z_SIZE):
            za_copy(o, z).start()

    for o in range(1, Z_SIZE):
        source = lax.rem(z + Z_SIZE - o, Z_SIZE)
        @pl.when(source < Z_OWNERS)
        def _():
            za_copy(o, source).wait_recv()

    def rows(xx, start, size):
        row = y_lo * Y_ROWS + xx * X_ROWS + start
        return final.at[pl.ds(pl.multiple_of(row, UNIT), size)]

    cut = 7 * UNIT
    mine = rows(x, 0, X_ROWS)
    a0 = send(mine, mine, xa_s.at[0], xa_r.at[0], dev_xr)
    a1 = send(mine, mine, xa_s.at[1], xa_r.at[1], dev_xl)
    b0 = send(mine, mine, ya_s.at[0], ya_r.at[0], dev_mate)
    a0.wait_recv()
    ring_lo = rows(x_l1, 0, cut)
    a2 = send(ring_lo, ring_lo, xa_s.at[2], xa_r.at[2], dev_xr)
    got = rows(x_l1, 0, X_ROWS)
    b1 = send(got, got, ya_s.at[1], ya_r.at[1], dev_mate)
    a1.wait_recv()
    ring_hi = rows(x_r1, cut, X_ROWS - cut)
    a3 = send(ring_hi, ring_hi, xa_s.at[3], xa_r.at[3], dev_xl)
    got = rows(x_r1, 0, X_ROWS)
    b2 = send(got, got, ya_s.at[2], ya_r.at[2], dev_mate)
    a2.wait_recv()
    a3.wait_recv()
    got = rows(x_op, 0, X_ROWS)
    b3 = send(got, got, ya_s.at[3], ya_r.at[3], dev_mate)
    for copy in (b0, b1, b2, b3):
        copy.wait_recv()

    tile_rows = o_ref.shape[0]
    for i in range(o_ref.shape[1] // LANES):
        o_ref[:, i * LANES : (i + 1) * LANES] = final[
            i * tile_rows : (i + 1) * tile_rows
        ].astype(jnp.float32)

    for copy in core_copies + [y0, y1, y2, y3, y4, y5, x0, x1, x2, x3, x4, x5]:
        copy.wait_send()
    for o in range(1, Z_SIZE):
        @pl.when(lax.rem(z + o, Z_SIZE) < Z_OWNERS)
        def _():
            z_copy(o).wait_send()

    @pl.when(z < Z_OWNERS)
    def _():
        for o in range(1, Z_SIZE):
            za_copy(o, z).wait_send()
    for copy in (a0, a1, a2, a3, b0, b1, b2, b3):
        copy.wait_send()


def reduce_gradients(packed, rows, cols):
    f32, bf16 = jnp.float32, jnp.bfloat16
    half, xh = Y_ROWS // 2, X_ROWS // 2
    dma = pltpu.SemaphoreType.DMA
    return pl.pallas_call(
        reduce_kernel,
        out_shape=jax.ShapeDtypeStruct((rows, cols), f32),
        in_specs=[pl.BlockSpec(memory_space=pltpu.VMEM)],
        out_specs=pl.BlockSpec(memory_space=pltpu.VMEM),
        scratch_shapes=[
            pltpu.VMEM((RING, Y_ROWS, LANES), f32),
            pltpu.VMEM((3, Y_ROWS, LANES), bf16),
            pltpu.VMEM((2, half, LANES), bf16),
            pltpu.VMEM((2, half, LANES), bf16),
            pltpu.VMEM((2, Y_ROWS, LANES), bf16),
            pltpu.VMEM((RING, X_ROWS, LANES), f32),
            pltpu.VMEM((2, xh, LANES), f32),
            pltpu.VMEM((2, xh, LANES), f32),
            pltpu.VMEM((2, X_ROWS, LANES), f32),
            pltpu.VMEM((Z_OWNERS, UNIT, LANES), f32),
            pltpu.VMEM((Z_SIZE - 1, UNIT, LANES), f32),
            pltpu.VMEM((Q_ROWS, LANES), bf16),
            dma((RING,)), dma((RING,)),
            dma((6,)), dma((6,)),
            dma((6,)), dma((6,)),
            dma((Z_SIZE - 1,)), dma((Z_SIZE - 1,)),
            dma((Z_SIZE - 1,)), dma((Z_SIZE - 1,)),
            dma((4,)), dma((4,)),
            dma((4,)), dma((4,)),
        ],
        compiler_params=pltpu.CompilerParams(
            collective_id=0, has_side_effects=True, vmem_limit_bytes=40 << 20
        ),
        name="reduce_gradients",
    )(packed)


def per_device(cached, send_rows, take_rows, utt_index, upstream, in_proj, norm_gain, conv_kernel):
    cache_rows = cached[0, 0]
    wanted = send_rows[0, 0]
    outgoing = cache_rows[jnp.maximum(wanted, 0)]
    proj_full, taps_full, gain_full = (
        lax.all_gather(in_proj, "fsdp", axis=1, tiled=True),
        lax.all_gather(conv_kernel, "fsdp", axis=1, tiled=True),
        lax.all_gather(norm_gain[None, :], "fsdp", axis=1, tiled=True),
    )
    take_list = take_rows[0, 0]
    slot = lax.iota(jnp.int32, take_list.shape[0])
    place = slot + GAP * utt_index[0, 0]
    order = lax.iota(jnp.int32, ROWS)
    position = (order % SUB) * SPAN + order // SUB
    held = (place[None, :] == position[:, None]) & (take_list >= 0)[None, :]
    source = jnp.max(jnp.where(held, slot[None, :], -1), axis=1)
    taken = jnp.max(jnp.where(held, take_list[None, :], -1), axis=1)
    live = source >= 0
    picked = jnp.maximum(source, 0) * 2
    steps = jnp.concatenate([picked, picked + 1])
    above = upstream[0, 0][steps]
    above = jnp.where(jnp.concatenate([live, live])[:, None], above, jnp.zeros((), above.dtype))
    arrived = lax.all_to_all(outgoing, "dp", split_axis=0, concat_axis=0, tiled=True)
    flat_rows = arrived.reshape(-1, arrived.shape[2])
    frames = jnp.where(
        live[:, None], flat_rows[jnp.maximum(taken, 0)], jnp.zeros((), flat_rows.dtype)
    )
    packed, device_loss = module_terms(frames, above, proj_full, gain_full, taps_full)
    depth, cols = in_proj.shape
    total = reduce_gradients(packed, depth + TAPS + 1, cols)
    return (
        total[:depth],
        total[depth : depth + TAPS],
        total[depth + TAPS],
        device_loss,
    )


def solution(mesh):
    placed = (
        P("dp", "fsdp", None, None),
        P("dp", "fsdp", None, None),
        P("dp", "fsdp", None),
        P("dp", "fsdp", None),
        P("dp", "fsdp", None, None),
        P(None, "fsdp"),
        P("fsdp"),
        P(None, "fsdp"),
    )
    return jax.shard_map(
        per_device,
        mesh=mesh,
        in_specs=placed,
        out_specs=(P(None, "fsdp"), P(None, "fsdp"), P("fsdp"), P("dp", "fsdp")),
        check_vma=False,
    )
```

```python
import functools

import jax
import jax.numpy as jnp
from jax import lax
from jax.experimental import pallas as pl
from jax.experimental.pallas import tpu as pltpu
from jax.sharding import PartitionSpec as P

LANES = 128
RING = 4
Z_SIZE = 16
UNIT = 16
Z_OWNERS = 13
X_ROWS = Z_OWNERS * UNIT
Y_ROWS = RING * X_ROWS
Q_ROWS = 2 * Y_ROWS
MESH_ID = pl.DeviceIdType.MESH


SUB = 8
SPAN = 42
HALO = 8
TAPS = 31
REACH = TAPS // 2
BLOCK = 7
GAP = 8
ROWS = SPAN * SUB


def module_kernel(fr_ref, up_ref, w_ref, gain_ref, taps_ref, out_ref, loss_ref,
                  x_s, xh_s, go_s, h_s, inv_s, gc_s, sh_s, shx_s, gx_s, ft_s):
    f32, bf16 = jnp.float32, jnp.bfloat16
    tiles = gain_ref.shape[0]
    width = tiles * LANES
    depth = w_ref.shape[0]
    scale = (2 * 256 * width) ** (-0.5)

    for h in range(2):
        frame = fr_ref[h * ROWS : (h + 1) * ROWS, :]
        ft_s[:, h * ROWS : (h + 1) * ROWS] = frame.T
        x_s[h] = jnp.dot(frame, w_ref[...], preferred_element_type=f32)

    def norm_rows(i, loss):
        for h in range(2):
            at = pl.ds(pl.multiple_of(i * 16, 16), 16)
            xv = x_s[h, at, :]
            mean = jnp.sum(xv, axis=1, keepdims=True) * (1.0 / width)
            cen = xv - mean
            var = jnp.sum(cen * cen, axis=1, keepdims=True) * (1.0 / width)
            inv = lax.rsqrt(var + 1e-05)
            inv_s[h, pl.ds(2 * i, 2)] = jnp.broadcast_to(inv, (16, LANES)).reshape(2, SUB, LANES)
            for c in range(tiles):
                lanes = slice(c * LANES, (c + 1) * LANES)
                up = up_ref[pl.ds(pl.multiple_of(h * ROWS + i * 16, 16), 16), lanes]
                go = up.astype(f32) * scale
                go_s[c, h, pl.ds(2 * i, 2)] = go.reshape(2, SUB, LANES)
                xh_s[c, h, pl.ds(HALO + 2 * i, 2)] = (cen[:, lanes] * inv).reshape(2, SUB, LANES)
                loss = loss + go * xv[:, lanes]
        return loss

    loss = lax.fori_loop(0, SPAN // 2, norm_rows, jnp.zeros((16, LANES), f32))
    loss = loss[:SUB] + loss[SUB:]

    sub = lax.broadcasted_iota(jnp.int32, (SUB, LANES), 0)

    def fill_halo(ref):
        for h in range(2):
            for j in range(HALO):
                before = pltpu.roll(ref[h, SPAN + j], 1, 0)
                ref[h, j] = jnp.where(sub == 0, 0.0, before)
                after = pltpu.roll(ref[h, HALO + j], SUB - 1, 0)
                ref[h, HALO + SPAN + j] = jnp.where(sub == SUB - 1, 0.0, after)

    spots = [(h, j) for j in range(BLOCK) for h in range(2)]

    def reach_of(h_in, m):
        found = []
        for h, j in spots:
            d = 2 * (m - j) + h_in - h
            if -REACH <= d <= REACH:
                found.append(((h, j), d + REACH))
        return found

    def conv_block(ref, taps, j0):
        accs = {}
        for m in range(-HALO, BLOCK + HALO):
            for h_in in range(2):
                uses = reach_of(h_in, m)
                if not uses:
                    continue
                v = ref[h_in, j0 + (HALO + m)]
                for spot, k in uses:
                    term = taps[k] * v
                    accs[spot] = accs[spot] + term if spot in accs else term
        return accs

    sh_s[...] = jnp.zeros_like(sh_s)
    shx_s[...] = jnp.zeros_like(shx_s)

    def channel_tile(ct, loss):
        xh = xh_s.at[ct]
        fill_halo(xh)
        gain = jnp.broadcast_to(gain_ref[ct], (SUB, LANES))

        def tap(k):
            return jnp.broadcast_to(taps_ref[ct, k : k + 1, :], (SUB, LANES))

        def forward(b, loss):
            j0 = b * BLOCK
            taps = [tap(k) * gain for k in range(TAPS)]
            accs = conv_block(xh, taps, j0)
            for (h, j), c in accs.items():
                sig = 1.0 / (1.0 + jnp.exp(-c))
                go = go_s[ct, h, j0 + j]
                gos = go * sig
                loss = loss + c * gos
                gc_s[h, j0 + (HALO + j)] = gos * (1.0 + c * (1.0 - sig))
            return loss

        loss = lax.fori_loop(0, SPAN // BLOCK, forward, loss)
        fill_halo(gc_s)

        def backward(b, gg):
            j0 = b * BLOCK
            taps = [tap(TAPS - 1 - k) for k in range(TAPS)]
            accs = conv_block(gc_s, taps, j0)
            for (h, j), gn in accs.items():
                v = xh[h, j0 + (HALO + j)]
                gg = gg + gn * v
                hv = gn * gain
                h_s[ct, h, j0 + j] = hv
                sh_s[h, j0 + j] = sh_s[h, j0 + j] + hv
                shx_s[h, j0 + j] = shx_s[h, j0 + j] + hv * v
            return gg

        zero = jnp.zeros((SUB, LANES), f32)
        gg = lax.fori_loop(0, SPAN // BLOCK, backward, zero)

        def tap_sums(b, sums):
            j0 = b * BLOCK
            sums = list(sums)
            gcs = {(h, j): gc_s[h, j0 + (HALO + j)] for h, j in spots}
            for m in range(-HALO, BLOCK + HALO):
                for h_in in range(2):
                    uses = reach_of(h_in, m)
                    if not uses:
                        continue
                    v = xh[h_in, j0 + (HALO + m)]
                    for spot, k in uses:
                        sums[k] = sums[k] + gcs[spot] * v
            return tuple(sums)

        sums = lax.fori_loop(0, SPAN // BLOCK, tap_sums, (zero,) * TAPS)
        base = lax.div(ct, 3) * Q_ROWS + lax.rem(ct, 3) * (depth + TAPS + 1) + depth
        gain_row = gain_ref[ct]
        tail = [jnp.sum(v, axis=0, keepdims=True) * gain_row for v in sums]
        tail.append(jnp.sum(gg, axis=0, keepdims=True))
        out_ref[pl.ds(pl.multiple_of(base, SUB), TAPS + 1), :] = jnp.concatenate(tail, axis=0)
        return loss

    loss = lax.fori_loop(0, tiles, channel_tile, loss)
    loss_ref[...] = jnp.sum(loss, keepdims=True)

    def grad_rows(i, carry):
        for h in range(2):
            two = pl.ds(2 * i, 2)
            mh = jnp.sum(sh_s[h, two], axis=2, keepdims=True) * (1.0 / width)
            mhx = jnp.sum(shx_s[h, two], axis=2, keepdims=True) * (1.0 / width)
            inv = inv_s[h, two]
            for c in range(tiles):
                xv = xh_s[c, h, pl.ds(HALO + 2 * i, 2)]
                gx = go_s[c, h, two] + inv * (h_s[c, h, two] - mh - xv * mhx)
                gx_s[pl.ds(pl.multiple_of(h * ROWS + i * 16, 16), 16), c * LANES : (c + 1) * LANES] = (
                    gx.reshape(16, LANES).astype(bf16)
                )
        return carry

    lax.fori_loop(0, SPAN // 2, grad_rows, 0)

    per = 2 * LANES
    for c in range(0, tiles, 2):
        gw = jnp.dot(ft_s[...], gx_s[:, c * LANES : c * LANES + per], preferred_element_type=f32)
        for k in range(2):
            base = (c + k) // 3 * Q_ROWS + (c + k) % 3 * (depth + TAPS + 1)
            out_ref[base : base + depth, :] = gw[:, k * LANES : (k + 1) * LANES]
    used = 3 * (depth + TAPS + 1)
    for q in range(tiles // 3):
        out_ref[q * Q_ROWS + used : (q + 1) * Q_ROWS, :] = jnp.zeros((Q_ROWS - used, LANES), f32)


def module_terms(frames, above, proj, tap_tiles, gain_tiles):
    f32, bf16 = jnp.float32, jnp.bfloat16
    tiles = proj.shape[1] // LANES
    depth = proj.shape[0]
    vm = pl.BlockSpec(memory_space=pltpu.VMEM)
    rows = (2, SPAN, SUB, LANES)
    return pl.pallas_call(
        module_kernel,
        out_shape=(
            jax.ShapeDtypeStruct((tiles // 3 * Q_ROWS, LANES), f32),
            jax.ShapeDtypeStruct((1, 1), f32),
        ),
        in_specs=[vm] * 5,
        out_specs=(vm, vm),
        scratch_shapes=[
            pltpu.VMEM((2, ROWS, tiles * LANES), f32),
            pltpu.VMEM((tiles, 2, SPAN + 2 * HALO, SUB, LANES), f32),
            pltpu.VMEM((tiles,) + rows, f32),
            pltpu.VMEM((tiles,) + rows, f32),
            pltpu.VMEM(rows, f32),
            pltpu.VMEM((2, SPAN + 2 * HALO, SUB, LANES), f32),
            pltpu.VMEM(rows, f32),
            pltpu.VMEM(rows, f32),
            pltpu.VMEM((2 * ROWS, tiles * LANES), bf16),
            pltpu.VMEM((depth, 2 * ROWS), bf16),
        ],
        compiler_params=pltpu.CompilerParams(vmem_limit_bytes=56 << 20),
        name="module_terms",
    )(frames, above, proj, gain_tiles, tap_tiles)


def exchange_kernel(
    cache_ref, want_ref, take_ref, utt_ref, tpos_ref, up_ref, w_ref, taps_ref, gain_ref,
    fr_ref, above_ref, proj_ref, tapt_ref, gaint_ref,
    pick_s, send_s, arr_s, taps_s, gain_s,
    row_s, row_r, par_s, par_r,
):
    f32, bf16 = jnp.float32, jnp.bfloat16
    peers = arr_s.shape[0]
    members = proj_ref.shape[1] // w_ref.shape[1]
    cols = w_ref.shape[1]
    p = lax.axis_index("dp")
    f = lax.axis_index("fsdp")

    def peer(o):
        return lax.rem(p + o, peers)

    barrier = pltpu.get_barrier_semaphore()

    def greet(o, carry):
        pl.semaphore_signal(barrier, inc=1, device_id=(peer(o), f), device_id_type=MESH_ID)
        return carry

    lax.fori_loop(1, peers, greet, 0)
    for o in range(1, members):
        pl.semaphore_signal(
            barrier, inc=1, device_id=(p, lax.rem(f + o, members)), device_id_type=MESH_ID
        )

    count, width = cache_ref.shape
    half = width // 2
    want = jnp.concatenate([want_ref[...], want_ref[...]], axis=0)
    cache_ids = lax.broadcasted_iota(jnp.int32, (SUB, count), 1)
    for d in range(0, peers, 2):
        two = [
            (jnp.broadcast_to(want[:, d + k : d + k + 1], (SUB, count)) == cache_ids).astype(f32)
            for k in range(2)
        ]
        pick_s[d * SUB : (d + 2) * SUB, :count] = jnp.concatenate(two, axis=0).astype(bf16)
    step = 256
    first = lax.broadcasted_iota(jnp.int32, (step, half), 0) % SUB < SUB // 2
    for r in range(0, peers * SUB, step):
        rows = jnp.dot(pick_s[r : r + step, :count], cache_ref[...], preferred_element_type=f32)
        rows = jnp.where(first, rows[:, :half], rows[:, half:])
        send_s[r // SUB : (r + step) // SUB] = rows.reshape(step // SUB, SUB, half).astype(bf16)

    pl.semaphore_wait(barrier, peers - 1 + members - 1)

    def row_copy(o):
        return pltpu.make_async_remote_copy(
            src_ref=send_s.at[peer(o)],
            dst_ref=arr_s.at[p],
            send_sem=row_s,
            recv_sem=row_r,
            device_id=(peer(o), f),
            device_id_type=MESH_ID,
        )

    def param_copies(o):
        lanes = pl.ds(pl.multiple_of(f * cols, LANES), cols)
        pairs = [(w_ref, proj_ref), (taps_ref, taps_s), (gain_ref, gain_s)]
        return [
            pltpu.make_async_remote_copy(
                src_ref=src,
                dst_ref=dst.at[:, lanes],
                send_sem=par_s.at[3 * (o - 1) + i],
                recv_sem=par_r.at[3 * (o - 1) + i],
                device_id=(p, lax.rem(f + o, members)),
                device_id_type=MESH_ID,
            )
            for i, (src, dst) in enumerate(pairs)
        ]

    row_copy(peers // 2).start()

    def start_rows(i, carry):
        o = peers // 2 - i
        row_copy(o).start()
        row_copy(peers - o).start()
        return carry

    lax.fori_loop(1, peers // 2, start_rows, 0)
    for o in range(1, members):
        for copy in param_copies(o):
            copy.start()
    arr_s[p] = send_s[p]
    own = pl.ds(pl.multiple_of(f * cols, LANES), cols)
    proj_ref[:, own] = w_ref[...]
    taps_s[:, own] = taps_ref[...]
    gain_s[:, own] = gain_ref[...]

    sub = lax.broadcasted_iota(jnp.int32, (SUB, 1), 0)
    steps = tpos_ref.shape[1]
    slots = take_ref.shape[1]
    place = lax.broadcasted_iota(jnp.int32, (1, slots), 1) + GAP * utt_ref[...]
    place = jnp.broadcast_to(place, (SUB, slots))
    take = jnp.broadcast_to(take_ref[...], (SUB, slots))
    tpos = jnp.broadcast_to(tpos_ref[...], (SUB, steps))
    for h in range(2):
        for j in range(0, SPAN, 2):
            two = [
                (tpos == 2 * (sub * SPAN + (j + k)) + h).astype(f32) for k in range(2)
            ]
            row = h * ROWS + j * SUB
            pick_s[row : row + 2 * SUB, :steps] = jnp.concatenate(two, axis=0).astype(bf16)
    for r in range(0, 2 * ROWS, ROWS // 2):
        above_ref[r : r + ROWS // 2, :] = jnp.dot(
            pick_s[r : r + ROWS // 2, :steps], up_ref[...], preferred_element_type=f32
        ).astype(bf16)
    arrived = lax.broadcasted_iota(jnp.int32, (SUB, peers * SUB), 1)
    for j in range(0, SPAN, 2):
        twos = ([], [])
        for k in range(2):
            held = place == sub * SPAN + (j + k)
            taken = jnp.max(jnp.where(held, take, -1), axis=1, keepdims=True)
            taken = jnp.where(taken < 0, -SUB, taken + taken // 4 * 4)
            for h in range(2):
                twos[h].append((jnp.broadcast_to(taken + 4 * h, arrived.shape) == arrived).astype(f32))
        for h in range(2):
            row = h * ROWS + j * SUB
            pick_s[row : row + 2 * SUB, :] = jnp.concatenate(twos[h], axis=0).astype(bf16)

    for o in range(1, members):
        for copy in param_copies(o):
            copy.wait_recv()
    tiles = gaint_ref.shape[0]
    for c in range(tiles):
        lanes = slice(c * LANES, (c + 1) * LANES)
        tapt_ref[c] = taps_s[:, lanes].astype(f32)
        gaint_ref[c] = gain_s[:, lanes].astype(f32)

    whole = pltpu.make_async_remote_copy(
        src_ref=send_s.at[pl.ds(0, peers - 1)],
        dst_ref=arr_s.at[pl.ds(0, peers - 1)],
        send_sem=row_s,
        recv_sem=row_r,
        device_id=(peer(1), f),
        device_id_type=MESH_ID,
    )
    whole.wait_recv()
    table = arr_s[...].astype(f32).reshape(peers * SUB, half).astype(bf16)
    for h in range(2):
        rows = slice(h * ROWS, (h + 1) * ROWS)
        fr_ref[rows, :] = jnp.dot(pick_s[rows, :], table, preferred_element_type=f32).astype(bf16)
    whole.wait_send()
    for o in range(1, members):
        for copy in param_copies(o):
            copy.wait_send()


def exchange(cache_rows, wanted, take, utt, upstream, in_proj, taps, gain, members):
    f32, bf16, i32 = jnp.float32, jnp.bfloat16, jnp.int32
    peers = wanted.shape[0]
    slots = take.shape[0]
    step = lax.iota(i32, 2 * slots)
    place = lax.iota(i32, slots) + GAP * utt
    tpos = jnp.where(
        jnp.repeat(take, 2) >= 0, 2 * jnp.repeat(place, 2) + step % 2, -1
    )
    depth, cols = in_proj.shape
    width = cols * members
    tiles = width // LANES
    half = cache_rows.shape[1] // 2
    vm = pl.BlockSpec(memory_space=pltpu.VMEM)
    dma = pltpu.SemaphoreType.DMA
    shape = jax.ShapeDtypeStruct
    return pl.pallas_call(
        exchange_kernel,
        out_shape=(
            shape((2 * ROWS, half), bf16),
            shape((2 * ROWS, width), bf16),
            shape((depth, width), bf16),
            shape((tiles, TAPS, LANES), f32),
            shape((tiles, 1, LANES), f32),
        ),
        in_specs=[vm] * 9,
        out_specs=(vm,) * 5,
        scratch_shapes=[
            pltpu.VMEM((max(2 * ROWS, peers * SUB), peers * SUB), bf16),
            pltpu.VMEM((peers, SUB, half), bf16),
            pltpu.VMEM((peers, SUB, half), bf16),
            pltpu.VMEM((TAPS, width), bf16),
            pltpu.VMEM((1, width), bf16),
            dma, dma,
            dma((3 * (members - 1),)), dma((3 * (members - 1),)),
        ],
        compiler_params=pltpu.CompilerParams(
            collective_id=1, has_side_effects=True, vmem_limit_bytes=40 << 20
        ),
        name="exchange",
    )(
        cache_rows, wanted.T, take[None, :], utt[None, :], tpos[None, :], upstream,
        in_proj, taps, gain[None, :],
    )


def reduce_kernel(
    g_ref, o_ref,
    cbuf, ysend, ystage, yfirst, yfrom,
    xbuf, xstage, xfirst, xfrom,
    zbuf, zfrom, final,
    core_s, core_r, y_s, y_r, x_s, x_r, z_s, z_r, za_s, za_r, xa_s, xa_r, ya_s, ya_r,
):
    p = lax.axis_index("dp")
    f = lax.axis_index("fsdp")
    x = lax.rem(p, RING)
    z = lax.rem(lax.div(p, RING), Z_SIZE)
    y_lo = lax.div(p, RING * Z_SIZE)
    y_hi = lax.div(f, 2)
    core = lax.rem(f, 2)
    y = y_hi * 2 + y_lo

    def at(yy, zz, xx, cc):
        return (
            (lax.rem(yy, 2) * Z_SIZE + zz) * RING + xx,
            lax.div(yy, 2) * 2 + cc,
        )

    y_r1, y_l1, y_op = lax.rem(y + 1, RING), lax.rem(y + 3, RING), lax.rem(y + 2, RING)
    x_r1, x_l1, x_op = lax.rem(x + 1, RING), lax.rem(x + 3, RING), lax.rem(x + 2, RING)
    y_mate = y_hi * 2 + 1 - y_lo
    dev_core = at(y, z, x, 1 - core)
    dev_yr, dev_yl = at(y_r1, z, x, core), at(y_l1, z, x, core)
    dev_xr, dev_xl = at(y, z, x_r1, core), at(y, z, x_l1, core)
    dev_mate = at(y_mate, z, x, core)

    def dev_z(o):
        return at(y, lax.rem(z + o, Z_SIZE), x, core)

    barrier = pltpu.get_barrier_semaphore()
    for d in [dev_core, dev_yr, dev_yl, dev_xr, dev_xl]:
        pl.semaphore_signal(barrier, inc=1, device_id=d, device_id_type=MESH_ID)
    for o in range(1, Z_SIZE):
        pl.semaphore_signal(barrier, inc=1, device_id=dev_z(o), device_id_type=MESH_ID)
    pl.semaphore_wait(barrier, 5 + Z_SIZE - 1)

    def send(src, dst, ssem, rsem, d):
        copy = pltpu.make_async_remote_copy(
            src_ref=src, dst_ref=dst, send_sem=ssem, recv_sem=rsem,
            device_id=d, device_id_type=MESH_ID,
        )
        copy.start()
        return copy

    def piece(yy, cc):
        row = (lax.div(yy, 2) * 2 + cc) * Q_ROWS + lax.rem(yy, 2) * Y_ROWS
        return pl.ds(pl.multiple_of(row, UNIT), Y_ROWS)

    core_copies = []
    for o in (2, 1, 3, 0):
        yy = lax.rem(y + o, RING)
        core_copies.append(
            send(g_ref.at[piece(yy, 1 - core)], cbuf.at[o], core_s.at[o], core_r.at[o], dev_core)
        )
    half = Y_ROWS // 2
    lo, hi = pl.ds(0, half), pl.ds(half, half)

    def summed(o):
        return g_ref[piece(lax.rem(y + o, RING), core)] + cbuf[o]

    core_copies[0].wait_recv()
    ysend[1] = summed(2).astype(jnp.bfloat16)
    y0 = send(ysend.at[1, lo], yfirst.at[0], y_s.at[0], y_r.at[0], dev_yr)
    y1 = send(ysend.at[1, hi], yfirst.at[1], y_s.at[1], y_r.at[1], dev_yl)
    core_copies[1].wait_recv()
    ysend[0] = summed(1).astype(jnp.bfloat16)
    y2 = send(ysend.at[0, hi], yfrom.at[0, hi], y_s.at[2], y_r.at[2], dev_yr)
    core_copies[2].wait_recv()
    ysend[2] = summed(3).astype(jnp.bfloat16)
    y3 = send(ysend.at[2, lo], yfrom.at[1, lo], y_s.at[3], y_r.at[3], dev_yl)
    core_copies[3].wait_recv()
    y0.wait_recv()
    part = g_ref[piece(y_r1, core)] + cbuf[1]
    ystage[0] = (part[:half] + yfirst[0].astype(jnp.float32)).astype(jnp.bfloat16)
    y4 = send(ystage.at[0], yfrom.at[0, lo], y_s.at[4], y_r.at[4], dev_yr)
    y1.wait_recv()
    part = g_ref[piece(y_l1, core)] + cbuf[3]
    ystage[1] = (part[half:] + yfirst[1].astype(jnp.float32)).astype(jnp.bfloat16)
    y5 = send(ystage.at[1], yfrom.at[1, hi], y_s.at[5], y_r.at[5], dev_yl)
    for copy in (y2, y3, y4, y5):
        copy.wait_recv()
    xbuf[...] = (
        summed(0) + yfrom[0].astype(jnp.float32) + yfrom[1].astype(jnp.float32)
    ).reshape(RING, X_ROWS, LANES)

    xh = X_ROWS // 2
    xlo, xhi = pl.ds(0, xh), pl.ds(xh, xh)
    x0 = send(xbuf.at[x_op, xlo], xfirst.at[0], x_s.at[0], x_r.at[0], dev_xr)
    x1 = send(xbuf.at[x_op, xhi], xfirst.at[1], x_s.at[1], x_r.at[1], dev_xl)
    x2 = send(xbuf.at[x_r1, xhi], xfrom.at[0, xhi], x_s.at[2], x_r.at[2], dev_xr)
    x3 = send(xbuf.at[x_l1, xlo], xfrom.at[1, xlo], x_s.at[3], x_r.at[3], dev_xl)
    x0.wait_recv()
    xstage[0] = xbuf[x_r1, xlo] + xfirst[0]
    x4 = send(xstage.at[0], xfrom.at[0, xlo], x_s.at[4], x_r.at[4], dev_xr)
    x1.wait_recv()
    xstage[1] = xbuf[x_l1, xhi] + xfirst[1]
    x5 = send(xstage.at[1], xfrom.at[1, xhi], x_s.at[5], x_r.at[5], dev_xl)
    for copy in (x2, x3, x4, x5):
        copy.wait_recv()
    zbuf[...] = (xbuf[x] + xfrom[0] + xfrom[1]).reshape(Z_OWNERS, UNIT, LANES)

    def z_copy(o):
        to = lax.rem(z + o, Z_SIZE)
        return pltpu.make_async_remote_copy(
            src_ref=zbuf.at[lax.min(to, Z_OWNERS - 1)],
            dst_ref=zfrom.at[o - 1],
            send_sem=z_s.at[o - 1],
            recv_sem=z_r.at[o - 1],
            device_id=dev_z(o),
            device_id_type=MESH_ID,
        )

    def own_rows(zz):
        row = y_lo * Y_ROWS + x * X_ROWS + lax.min(zz, Z_OWNERS - 1) * UNIT
        return final.at[pl.ds(pl.multiple_of(row, UNIT), UNIT)]

    def za_copy(o, zz):
        return pltpu.make_async_remote_copy(
            src_ref=own_rows(zz),
            dst_ref=own_rows(zz),
            send_sem=za_s.at[o - 1],
            recv_sem=za_r.at[o - 1],
            device_id=dev_z(o),
            device_id_type=MESH_ID,
        )

    for o in range(1, Z_SIZE):
        @pl.when(lax.rem(z + o, Z_SIZE) < Z_OWNERS)
        def _():
            z_copy(o).start()

    @pl.when(z < Z_OWNERS)
    def _():
        total = zbuf[lax.min(z, Z_OWNERS - 1)]
        for o in range(1, Z_SIZE):
            z_copy(o).wait_recv()
            total = total + zfrom[o - 1]
        row = y_lo * Y_ROWS + x * X_ROWS + lax.min(z, Z_OWNERS - 1) * UNIT
        final[pl.ds(pl.multiple_of(row, UNIT), UNIT)] = total.astype(jnp.bfloat16)
        for o in range(1, Z_SIZE):
            za_copy(o, z).start()

    for o in range(1, Z_SIZE):
        source = lax.rem(z + Z_SIZE - o, Z_SIZE)
        @pl.when(source < Z_OWNERS)
        def _():
            za_copy(o, source).wait_recv()

    def rows(xx, start, size):
        row = y_lo * Y_ROWS + xx * X_ROWS + start
        return final.at[pl.ds(pl.multiple_of(row, UNIT), size)]

    cut = 7 * UNIT
    mine = rows(x, 0, X_ROWS)
    a0 = send(mine, mine, xa_s.at[0], xa_r.at[0], dev_xr)
    a1 = send(mine, mine, xa_s.at[1], xa_r.at[1], dev_xl)
    b0 = send(mine, mine, ya_s.at[0], ya_r.at[0], dev_mate)
    a0.wait_recv()
    ring_lo = rows(x_l1, 0, cut)
    a2 = send(ring_lo, ring_lo, xa_s.at[2], xa_r.at[2], dev_xr)
    got = rows(x_l1, 0, X_ROWS)
    b1 = send(got, got, ya_s.at[1], ya_r.at[1], dev_mate)
    a1.wait_recv()
    ring_hi = rows(x_r1, cut, X_ROWS - cut)
    a3 = send(ring_hi, ring_hi, xa_s.at[3], xa_r.at[3], dev_xl)
    got = rows(x_r1, 0, X_ROWS)
    b2 = send(got, got, ya_s.at[2], ya_r.at[2], dev_mate)
    a2.wait_recv()
    a3.wait_recv()
    got = rows(x_op, 0, X_ROWS)
    b3 = send(got, got, ya_s.at[3], ya_r.at[3], dev_mate)
    for copy in (b0, b1, b2, b3):
        copy.wait_recv()

    tile_rows = o_ref.shape[0]
    for i in range(o_ref.shape[1] // LANES):
        o_ref[:, i * LANES : (i + 1) * LANES] = final[
            i * tile_rows : (i + 1) * tile_rows
        ].astype(jnp.float32)

    for copy in core_copies + [y0, y1, y2, y3, y4, y5, x0, x1, x2, x3, x4, x5]:
        copy.wait_send()
    for o in range(1, Z_SIZE):
        @pl.when(lax.rem(z + o, Z_SIZE) < Z_OWNERS)
        def _():
            z_copy(o).wait_send()

    @pl.when(z < Z_OWNERS)
    def _():
        for o in range(1, Z_SIZE):
            za_copy(o, z).wait_send()
    for copy in (a0, a1, a2, a3, b0, b1, b2, b3):
        copy.wait_send()


def reduce_gradients(packed, rows, cols):
    f32, bf16 = jnp.float32, jnp.bfloat16
    half, xh = Y_ROWS // 2, X_ROWS // 2
    dma = pltpu.SemaphoreType.DMA
    return pl.pallas_call(
        reduce_kernel,
        out_shape=jax.ShapeDtypeStruct((rows, cols), f32),
        in_specs=[pl.BlockSpec(memory_space=pltpu.VMEM)],
        out_specs=pl.BlockSpec(memory_space=pltpu.VMEM),
        scratch_shapes=[
            pltpu.VMEM((RING, Y_ROWS, LANES), f32),
            pltpu.VMEM((3, Y_ROWS, LANES), bf16),
            pltpu.VMEM((2, half, LANES), bf16),
            pltpu.VMEM((2, half, LANES), bf16),
            pltpu.VMEM((2, Y_ROWS, LANES), bf16),
            pltpu.VMEM((RING, X_ROWS, LANES), f32),
            pltpu.VMEM((2, xh, LANES), f32),
            pltpu.VMEM((2, xh, LANES), f32),
            pltpu.VMEM((2, X_ROWS, LANES), f32),
            pltpu.VMEM((Z_OWNERS, UNIT, LANES), f32),
            pltpu.VMEM((Z_SIZE - 1, UNIT, LANES), f32),
            pltpu.VMEM((Q_ROWS, LANES), bf16),
            dma((RING,)), dma((RING,)),
            dma((6,)), dma((6,)),
            dma((6,)), dma((6,)),
            dma((Z_SIZE - 1,)), dma((Z_SIZE - 1,)),
            dma((Z_SIZE - 1,)), dma((Z_SIZE - 1,)),
            dma((4,)), dma((4,)),
            dma((4,)), dma((4,)),
        ],
        compiler_params=pltpu.CompilerParams(
            collective_id=0, has_side_effects=True, vmem_limit_bytes=40 << 20
        ),
        name="reduce_gradients",
    )(packed)


def per_device(
    members, cached, send_rows, take_rows, utt_index, upstream, in_proj, norm_gain, conv_kernel
):
    moved = exchange(
        cached[0, 0], send_rows[0, 0], take_rows[0, 0], utt_index[0, 0], upstream[0, 0],
        in_proj, conv_kernel, norm_gain, members,
    )
    packed, device_loss = module_terms(*moved)
    depth, cols = in_proj.shape
    total = reduce_gradients(packed, depth + TAPS + 1, cols)
    return (
        total[:depth],
        total[depth : depth + TAPS],
        total[depth + TAPS],
        device_loss,
    )


def solution(mesh):
    placed = (
        P("dp", "fsdp", None, None),
        P("dp", "fsdp", None, None),
        P("dp", "fsdp", None),
        P("dp", "fsdp", None),
        P("dp", "fsdp", None, None),
        P(None, "fsdp"),
        P("fsdp"),
        P(None, "fsdp"),
    )
    return jax.shard_map(
        functools.partial(per_device, mesh.shape["fsdp"]),
        mesh=mesh,
        in_specs=placed,
        out_specs=(P(None, "fsdp"), P(None, "fsdp"), P("fsdp"), P("dp", "fsdp")),
        check_vma=False,
    )
```

```python
import functools

import jax
import jax.numpy as jnp
from jax import lax
from jax.experimental import pallas as pl
from jax.experimental.pallas import tpu as pltpu
from jax.sharding import PartitionSpec as P

LANES = 128
RING = 4
Z_SIZE = 16
UNIT = 16
Z_OWNERS = 13
X_ROWS = Z_OWNERS * UNIT
Y_ROWS = RING * X_ROWS
Q_ROWS = 2 * Y_ROWS
MESH_ID = pl.DeviceIdType.MESH


SUB = 8
SPAN = 42
HALO = 8
TAPS = 31
REACH = TAPS // 2
BLOCK = 14
GAP = 8
ROWS = SPAN * SUB


def module_kernel(fr_hbm, up_hbm, w_hbm, gain_hbm, taps_hbm, out_ref, loss_ref,
                  x_s, xh_s, go_s, h_s, inv_s, gc_s, sh_s, shx_s, gx_s, ft_s,
                  tb_s, cx_s, cg_s, p_s, q_s,
                  fr_ref, up_ref, w_ref, gain_ref, taps_ref, in_sem):
    f32, bf16 = jnp.float32, jnp.bfloat16
    loads = [
        pltpu.make_async_copy(src, dst, in_sem.at[i])
        for i, (src, dst) in enumerate(
            [
                (w_hbm, w_ref), (fr_hbm, fr_ref), (up_hbm, up_ref),
                (gain_hbm, gain_ref), (taps_hbm, taps_ref),
            ]
        )
    ]
    for load in loads:
        load.start()
    loads[0].wait()
    loads[1].wait()
    tiles = gain_ref.shape[0]
    width = tiles * LANES
    depth = w_ref.shape[0]
    scale = (2 * 256 * width) ** (-0.5)

    for h in range(2):
        frame = fr_ref[h * ROWS : (h + 1) * ROWS, :]
        ft_s[:, h * ROWS : (h + 1) * ROWS] = frame.T
        x_s[h] = jnp.dot(frame, w_ref[...], preferred_element_type=f32)

    for load in loads[2:]:
        load.wait()

    def norm_rows(i, loss):
        for h in range(2):
            at = pl.ds(pl.multiple_of(i * 16, 16), 16)
            xv = x_s[h, at, :]
            mean = jnp.sum(xv, axis=1, keepdims=True) * (1.0 / width)
            cen = xv - mean
            var = jnp.sum(cen * cen, axis=1, keepdims=True) * (1.0 / width)
            inv = lax.rsqrt(var + 1e-05)
            inv_s[h, pl.ds(2 * i, 2)] = jnp.broadcast_to(inv, (16, LANES)).reshape(2, SUB, LANES)
            for c in range(tiles):
                lanes = slice(c * LANES, (c + 1) * LANES)
                up = up_ref[pl.ds(pl.multiple_of(h * ROWS + i * 16, 16), 16), lanes]
                go = up.astype(f32) * scale
                go_s[c, h, pl.ds(2 * i, 2)] = go.reshape(2, SUB, LANES)
                xh_s[c, h, pl.ds(HALO + 2 * i, 2)] = (cen[:, lanes] * inv).reshape(2, SUB, LANES)
                loss = loss + go * xv[:, lanes]
        return loss

    loss = lax.fori_loop(0, SPAN // 2, norm_rows, jnp.zeros((16, LANES), f32))
    loss = loss[:SUB] + loss[SUB:]

    sub = lax.broadcasted_iota(jnp.int32, (SUB, LANES), 0)

    def fill_halo(ref):
        for h in range(2):
            for j in range(HALO):
                before = pltpu.roll(ref[h, SPAN + j], 1, 0)
                ref[h, j] = jnp.where(sub == 0, 0.0, before)
                after = pltpu.roll(ref[h, HALO + j], SUB - 1, 0)
                ref[h, HALO + SPAN + j] = jnp.where(sub == SUB - 1, 0.0, after)

    evens = range(-(REACH // 2), REACH // 2 + 1)
    odds = range(-(REACH // 2) - 1, REACH // 2 + 1)

    def even_tap(m):
        return 2 * m + REACH

    def odd_tap(m):
        return 2 * m + 1 + REACH

    def slide(get, taps, j0):
        accs = {}
        for i in range(min(taps), BLOCK + max(taps)):
            v = get(j0 + (HALO + i))
            for j in range(BLOCK):
                if i - j in taps:
                    term = taps[i - j] * v
                    accs[j] = accs[j] + term if j in accs else term
        return accs

    def cross_sums(ref, cross):
        for j in range(2 * HALO + SPAN - 1):
            cross[j] = ref[1, j] + ref[0, j + 1]

    def conv(ref, cross, tap, use, carry):
        def parts(b, c):
            j0 = b * BLOCK
            own = slide(lambda j: ref[0, j], {m: tap(even_tap(m)) for m in evens}, j0)
            for j, v in own.items():
                p_s[j0 + j] = v
            own = slide(lambda j: ref[1, j], {m: tap(odd_tap(m)) for m in odds}, j0)
            for j, v in own.items():
                q_s[j0 + j] = v
            return c

        lax.fori_loop(0, SPAN // BLOCK, parts, 0)
        cross_sums(ref, cross)
        p_s[SPAN] = jnp.where(sub == SUB - 1, 0.0, pltpu.roll(p_s[0], SUB - 1, 0))

        def joined(b, carry):
            j0 = b * BLOCK
            both = {}
            for m in odds:
                both[m] = tap(odd_tap(m)) + tap(even_tap(m)) if m in evens else tap(odd_tap(m))
            third = slide(lambda j: cross[j], both, j0)
            for j in range(BLOCK):
                q = q_s[j0 + j]
                carry = use(0, j0 + j, p_s[j0 + j] + q, carry)
                carry = use(1, j0 + j, third[j] - (p_s[j0 + (j + 1)] + q), carry)
            return carry

        return lax.fori_loop(0, SPAN // BLOCK, joined, carry)

    sh_s[...] = jnp.zeros_like(sh_s)
    shx_s[...] = jnp.zeros_like(shx_s)

    def channel_tile(ct, loss):
        xh = xh_s.at[ct]
        fill_halo(xh)
        gain = jnp.broadcast_to(gain_ref[ct], (SUB, LANES))
        for k in range(TAPS):
            tap = jnp.broadcast_to(taps_ref[ct, k : k + 1, :], (SUB, LANES))
            tb_s[0, k] = tap * gain
            tb_s[1, TAPS - 1 - k] = tap

        def forward(h, j, c, loss):
            sig = 1.0 / (1.0 + jnp.exp(-c))
            gos = go_s[ct, h, j] * sig
            gc_s[h, j + HALO] = gos * (1.0 + c * (1.0 - sig))
            return loss + c * gos

        loss = conv(xh, cx_s, lambda k: tb_s[0, k], forward, loss)
        fill_halo(gc_s)

        def backward(h, j, gn, gg):
            v = xh[h, j + HALO]
            hv = gn * gain
            h_s[ct, h, j] = hv
            sh_s[h, j] = sh_s[h, j] + hv
            shx_s[h, j] = shx_s[h, j] + hv * v
            return gg + gn * v

        zero = jnp.zeros((SUB, LANES), f32)
        gg = conv(gc_s, cg_s, lambda k: tb_s[1, k], backward, zero)

        def correlate(grad, get, offsets):
            def block(b, sums):
                j0 = b * BLOCK
                sums = dict(zip(offsets, sums))
                grads = [grad(j0 + (HALO + j)) for j in range(BLOCK)]
                for i in range(offsets[0], BLOCK + offsets[-1]):
                    v = get(j0 + (HALO + i))
                    for j in range(BLOCK):
                        if i - j in sums:
                            sums[i - j] = sums[i - j] + grads[j] * v
                return tuple(sums[m] for m in offsets)

            sums = lax.fori_loop(0, SPAN // BLOCK, block, (zero,) * len(offsets))
            return dict(zip(offsets, sums))

        even = correlate(lambda j: gc_s[0, j] - gc_s[1, j - 1], lambda j: xh[0, j], evens)
        for m in evens:
            tb_s[0, even_tap(m)] = even[m]
        odd = correlate(lambda j: gc_s[0, j] - gc_s[1, j], lambda j: xh[1, j], odds)
        for m in odds:
            tb_s[0, odd_tap(m)] = odd[m]
        both = correlate(lambda j: gc_s[1, j], lambda j: cx_s[j], odds)
        for m in odds:
            tb_s[0, odd_tap(m)] = tb_s[0, odd_tap(m)] + both[m]
            if m in evens:
                tb_s[0, even_tap(m)] = tb_s[0, even_tap(m)] + both[m]
        base = lax.div(ct, 3) * Q_ROWS + lax.rem(ct, 3) * (depth + TAPS + 1) + depth
        gain_row = gain_ref[ct]
        tail = [jnp.sum(tb_s[0, k], axis=0, keepdims=True) * gain_row for k in range(TAPS)]
        tail.append(jnp.sum(gg, axis=0, keepdims=True))
        out_ref[pl.ds(pl.multiple_of(base, SUB), TAPS + 1), :] = jnp.concatenate(tail, axis=0)
        return loss

    loss = lax.fori_loop(0, tiles, channel_tile, loss)
    loss_ref[...] = jnp.sum(loss, keepdims=True)

    def grad_rows(i, carry):
        for h in range(2):
            two = pl.ds(2 * i, 2)
            mh = jnp.sum(sh_s[h, two], axis=2, keepdims=True) * (1.0 / width)
            mhx = jnp.sum(shx_s[h, two], axis=2, keepdims=True) * (1.0 / width)
            inv = inv_s[h, two]
            for c in range(tiles):
                xv = xh_s[c, h, pl.ds(HALO + 2 * i, 2)]
                gx = go_s[c, h, two] + inv * (h_s[c, h, two] - mh - xv * mhx)
                gx_s[pl.ds(pl.multiple_of(h * ROWS + i * 16, 16), 16), c * LANES : (c + 1) * LANES] = (
                    gx.reshape(16, LANES).astype(bf16)
                )
        return carry

    lax.fori_loop(0, SPAN // 2, grad_rows, 0)

    per = 2 * LANES
    for c in range(0, tiles, 2):
        gw = jnp.dot(ft_s[...], gx_s[:, c * LANES : c * LANES + per], preferred_element_type=f32)
        for k in range(2):
            base = (c + k) // 3 * Q_ROWS + (c + k) % 3 * (depth + TAPS + 1)
            out_ref[base : base + depth, :] = gw[:, k * LANES : (k + 1) * LANES]
    used = 3 * (depth + TAPS + 1)
    for q in range(tiles // 3):
        out_ref[q * Q_ROWS + used : (q + 1) * Q_ROWS, :] = jnp.zeros((Q_ROWS - used, LANES), f32)


def module_terms(frames, above, proj, tap_tiles, gain_tiles):
    f32, bf16 = jnp.float32, jnp.bfloat16
    tiles = proj.shape[1] // LANES
    depth = proj.shape[0]
    vm = pl.BlockSpec(memory_space=pltpu.VMEM)
    rows = (2, SPAN, SUB, LANES)
    return pl.pallas_call(
        module_kernel,
        out_shape=(
            jax.ShapeDtypeStruct((tiles // 3 * Q_ROWS, LANES), f32),
            jax.ShapeDtypeStruct((1, 1), f32),
        ),
        in_specs=[pl.BlockSpec(memory_space=pltpu.HBM)] * 5,
        out_specs=(vm, vm),
        scratch_shapes=[
            pltpu.VMEM((2, ROWS, tiles * LANES), f32),
            pltpu.VMEM((tiles, 2, SPAN + 2 * HALO, SUB, LANES), f32),
            pltpu.VMEM((tiles,) + rows, f32),
            pltpu.VMEM((tiles,) + rows, f32),
            pltpu.VMEM(rows, f32),
            pltpu.VMEM((2, SPAN + 2 * HALO, SUB, LANES), f32),
            pltpu.VMEM(rows, f32),
            pltpu.VMEM(rows, f32),
            pltpu.VMEM((2 * ROWS, tiles * LANES), bf16),
            pltpu.VMEM((depth, 2 * ROWS), bf16),
            pltpu.VMEM((2, TAPS, SUB, LANES), f32),
            pltpu.VMEM((SPAN + 2 * HALO, SUB, LANES), f32),
            pltpu.VMEM((SPAN + 2 * HALO, SUB, LANES), f32),
            pltpu.VMEM((SPAN + 1, SUB, LANES), f32),
            pltpu.VMEM((SPAN, SUB, LANES), f32),
            pltpu.VMEM(frames.shape, bf16),
            pltpu.VMEM(above.shape, bf16),
            pltpu.VMEM(proj.shape, bf16),
            pltpu.VMEM(gain_tiles.shape, f32),
            pltpu.VMEM(tap_tiles.shape, f32),
            pltpu.SemaphoreType.DMA((5,)),
        ],
        compiler_params=pltpu.CompilerParams(vmem_limit_bytes=56 << 20),
        name="module_terms",
    )(frames, above, proj, gain_tiles, tap_tiles)


def exchange_kernel(
    cache_hbm, want_hbm, take_hbm, utt_hbm, up_hbm, w_ref, taps_ref, gain_ref,
    fr_ref, above_ref, proj_ref, tapt_ref, gaint_ref,
    pick_s, send_s, arr_s, taps_s, gain_s,
    cache_ref, want_ref, take_ref, utt_ref, up_ref,
    row_s, row_r, par_s, par_r, in_sem,
):
    f32, bf16 = jnp.float32, jnp.bfloat16
    peers = arr_s.shape[0]
    members = proj_ref.shape[1] // w_ref.shape[1]
    cols = w_ref.shape[1]
    p = lax.axis_index("dp")
    f = lax.axis_index("fsdp")

    def peer(o):
        return lax.rem(p + o, peers)

    own = pl.ds(pl.multiple_of(f * cols, LANES), cols)
    loads = [
        pltpu.make_async_copy(src, dst, in_sem.at[i])
        for i, (src, dst) in enumerate(
            [
                (want_hbm, want_ref), (cache_hbm, cache_ref), (take_hbm, take_ref),
                (utt_hbm, utt_ref), (up_hbm, up_ref), (w_ref, proj_ref.at[:, own]),
                (taps_ref, taps_s.at[:, own]), (gain_ref, gain_s.at[:, own]),
            ]
        )
    ]
    for load in loads:
        load.start()

    barrier = pltpu.get_barrier_semaphore()

    def greet(o, carry):
        pl.semaphore_signal(barrier, inc=1, device_id=(peer(o), f), device_id_type=MESH_ID)
        return carry

    lax.fori_loop(1, peers, greet, 0)
    for o in range(1, members):
        pl.semaphore_signal(
            barrier, inc=1, device_id=(p, lax.rem(f + o, members)), device_id_type=MESH_ID
        )

    count, width = cache_ref.shape
    half = width // 2
    loads[0].wait()
    loads[1].wait()
    want = jnp.concatenate([want_ref[...], want_ref[...]], axis=0)
    cache_ids = lax.broadcasted_iota(jnp.int32, (SUB, count), 1)
    for d in range(0, peers, 2):
        two = [
            (jnp.broadcast_to(want[:, d + k : d + k + 1], (SUB, count)) == cache_ids).astype(f32)
            for k in range(2)
        ]
        pick_s[d * SUB : (d + 2) * SUB, :count] = jnp.concatenate(two, axis=0).astype(bf16)
    step = 256
    first = lax.broadcasted_iota(jnp.int32, (step, half), 0) % SUB < SUB // 2
    for r in range(0, peers * SUB, step):
        rows = jnp.dot(pick_s[r : r + step, :count], cache_ref[...], preferred_element_type=f32)
        rows = jnp.where(first, rows[:, :half], rows[:, half:])
        send_s[r // SUB : (r + step) // SUB] = rows.reshape(step // SUB, SUB, half).astype(bf16)

    pl.semaphore_wait(barrier, peers - 1 + members - 1)

    def row_copy(o):
        return pltpu.make_async_remote_copy(
            src_ref=send_s.at[peer(o)],
            dst_ref=arr_s.at[p],
            send_sem=row_s,
            recv_sem=row_r,
            device_id=(peer(o), f),
            device_id_type=MESH_ID,
        )

    def param_copies(o):
        lanes = pl.ds(pl.multiple_of(f * cols, LANES), cols)
        pairs = [(w_ref, proj_ref), (taps_ref, taps_s), (gain_ref, gain_s)]
        return [
            pltpu.make_async_remote_copy(
                src_ref=src,
                dst_ref=dst.at[:, lanes],
                send_sem=par_s.at[3 * (o - 1) + i],
                recv_sem=par_r.at[3 * (o - 1) + i],
                device_id=(p, lax.rem(f + o, members)),
                device_id_type=MESH_ID,
            )
            for i, (src, dst) in enumerate(pairs)
        ]

    row_copy(peers // 2).start()

    def start_rows(i, carry):
        o = peers // 2 - i
        row_copy(o).start()
        row_copy(peers - o).start()
        return carry

    lax.fori_loop(1, peers // 2, start_rows, 0)
    for o in range(1, members):
        for copy in param_copies(o):
            copy.start()
    arr_s[p] = send_s[p]
    for load in loads[2:]:
        load.wait()

    sub = lax.broadcasted_iota(jnp.int32, (SUB, 1), 0)
    steps = up_ref.shape[0]
    slots = take_ref.shape[1]
    place = lax.broadcasted_iota(jnp.int32, (1, slots), 1) + GAP * utt_ref[...]
    place = jnp.broadcast_to(jnp.where(take_ref[...] >= 0, place, -1), (SUB, slots))
    take = jnp.broadcast_to(take_ref[...], (SUB, slots))
    for j in range(0, SPAN, 2):
        two = [(place == sub * SPAN + (j + k)).astype(f32) for k in range(2)]
        pick_s[j * SUB : (j + 2) * SUB, steps : steps + slots] = (
            jnp.concatenate(two, axis=0).astype(bf16)
        )
    slot_ids = lax.broadcasted_iota(jnp.int32, (slots, steps), 0)
    step_ids = lax.broadcasted_iota(jnp.int32, (slots, steps), 1)
    for h in range(2):
        spread = (step_ids == 2 * slot_ids + h).astype(f32).astype(bf16)
        pick_s[h * ROWS : (h + 1) * ROWS, :steps] = jnp.dot(
            pick_s[:ROWS, steps : steps + slots], spread, preferred_element_type=f32
        ).astype(bf16)
    for r in range(0, 2 * ROWS, ROWS // 2):
        above_ref[r : r + ROWS // 2, :] = jnp.dot(
            pick_s[r : r + ROWS // 2, :steps], up_ref[...], preferred_element_type=f32
        ).astype(bf16)
    arrived = lax.broadcasted_iota(jnp.int32, (SUB, peers * SUB), 1)
    for j in range(0, SPAN, 2):
        twos = ([], [])
        for k in range(2):
            held = place == sub * SPAN + (j + k)
            taken = jnp.max(jnp.where(held, take, -1), axis=1, keepdims=True)
            taken = jnp.where(taken < 0, -SUB, taken + taken // 4 * 4)
            for h in range(2):
                twos[h].append((jnp.broadcast_to(taken + 4 * h, arrived.shape) == arrived).astype(f32))
        for h in range(2):
            row = h * ROWS + j * SUB
            pick_s[row : row + 2 * SUB, :] = jnp.concatenate(twos[h], axis=0).astype(bf16)

    for o in range(1, members):
        for copy in param_copies(o):
            copy.wait_recv()
    tiles = gaint_ref.shape[0]
    for c in range(tiles):
        lanes = slice(c * LANES, (c + 1) * LANES)
        tapt_ref[c] = taps_s[:, lanes].astype(f32)
        gaint_ref[c] = gain_s[:, lanes].astype(f32)

    whole = pltpu.make_async_remote_copy(
        src_ref=send_s.at[pl.ds(0, peers - 1)],
        dst_ref=arr_s.at[pl.ds(0, peers - 1)],
        send_sem=row_s,
        recv_sem=row_r,
        device_id=(peer(1), f),
        device_id_type=MESH_ID,
    )
    whole.wait_recv()
    table = arr_s[...].astype(f32).reshape(peers * SUB, half).astype(bf16)
    for h in range(2):
        rows = slice(h * ROWS, (h + 1) * ROWS)
        fr_ref[rows, :] = jnp.dot(pick_s[rows, :], table, preferred_element_type=f32).astype(bf16)
    whole.wait_send()
    for o in range(1, members):
        for copy in param_copies(o):
            copy.wait_send()


def exchange(cache_rows, wanted, take, utt, upstream, in_proj, taps, gain, members):
    f32, bf16, i32 = jnp.float32, jnp.bfloat16, jnp.int32
    peers = wanted.shape[0]
    slots = take.shape[0]
    depth, cols = in_proj.shape
    width = cols * members
    tiles = width // LANES
    half = cache_rows.shape[1] // 2
    vm = pl.BlockSpec(memory_space=pltpu.VMEM)
    dma = pltpu.SemaphoreType.DMA
    shape = jax.ShapeDtypeStruct
    return pl.pallas_call(
        exchange_kernel,
        out_shape=(
            shape((2 * ROWS, half), bf16),
            shape((2 * ROWS, width), bf16),
            shape((depth, width), bf16),
            shape((tiles, TAPS, LANES), f32),
            shape((tiles, 1, LANES), f32),
        ),
        in_specs=[pl.BlockSpec(memory_space=pltpu.HBM)] * 8,
        out_specs=(vm,) * 5,
        scratch_shapes=[
            pltpu.VMEM((max(2 * ROWS, peers * SUB), peers * SUB), bf16),
            pltpu.VMEM((peers, SUB, half), bf16),
            pltpu.VMEM((peers, SUB, half), bf16),
            pltpu.VMEM((TAPS, width), bf16),
            pltpu.VMEM((1, width), bf16),
            pltpu.VMEM(cache_rows.shape, bf16),
            pltpu.VMEM(wanted.shape[::-1], i32),
            pltpu.VMEM((1, slots), i32),
            pltpu.VMEM((1, slots), i32),
            pltpu.VMEM(upstream.shape, bf16),
            dma, dma,
            dma((3 * (members - 1),)), dma((3 * (members - 1),)),
            dma((8,)),
        ],
        compiler_params=pltpu.CompilerParams(
            collective_id=1, has_side_effects=True, vmem_limit_bytes=56 << 20
        ),
        name="exchange",
    )(
        cache_rows, wanted.T, take[None, :], utt[None, :], upstream,
        in_proj, taps, gain[None, :],
    )


def reduce_kernel(
    g_ref, o_ref,
    gown, own_sem, cbuf, ysend, ystage, yfirst, yfrom,
    xbuf, xstage, xfirst, xfrom,
    zbuf, zfrom, final,
    core_s, core_r, y_s, y_r, x_s, x_r, z_s, z_r, za_s, za_r, xa_s, xa_r, ya_s, ya_r,
):
    p = lax.axis_index("dp")
    f = lax.axis_index("fsdp")
    x = lax.rem(p, RING)
    z = lax.rem(lax.div(p, RING), Z_SIZE)
    y_lo = lax.div(p, RING * Z_SIZE)
    y_hi = lax.div(f, 2)
    core = lax.rem(f, 2)
    y = y_hi * 2 + y_lo

    def at(yy, zz, xx, cc):
        return (
            (lax.rem(yy, 2) * Z_SIZE + zz) * RING + xx,
            lax.div(yy, 2) * 2 + cc,
        )

    y_r1, y_l1, y_op = lax.rem(y + 1, RING), lax.rem(y + 3, RING), lax.rem(y + 2, RING)
    x_r1, x_l1, x_op = lax.rem(x + 1, RING), lax.rem(x + 3, RING), lax.rem(x + 2, RING)
    y_mate = y_hi * 2 + 1 - y_lo
    dev_core = at(y, z, x, 1 - core)
    dev_yr, dev_yl = at(y_r1, z, x, core), at(y_l1, z, x, core)
    dev_xr, dev_xl = at(y, z, x_r1, core), at(y, z, x_l1, core)
    dev_mate = at(y_mate, z, x, core)

    def dev_z(o):
        return at(y, lax.rem(z + o, Z_SIZE), x, core)

    barrier = pltpu.get_barrier_semaphore()
    for d in [dev_core, dev_yr, dev_yl, dev_xr, dev_xl]:
        pl.semaphore_signal(barrier, inc=1, device_id=d, device_id_type=MESH_ID)
    for o in range(1, Z_SIZE):
        pl.semaphore_signal(barrier, inc=1, device_id=dev_z(o), device_id_type=MESH_ID)
    pl.semaphore_wait(barrier, 5 + Z_SIZE - 1)

    def send(src, dst, ssem, rsem, d):
        copy = pltpu.make_async_remote_copy(
            src_ref=src, dst_ref=dst, send_sem=ssem, recv_sem=rsem,
            device_id=d, device_id_type=MESH_ID,
        )
        copy.start()
        return copy

    def piece(yy, cc):
        row = (lax.div(yy, 2) * 2 + cc) * Q_ROWS + lax.rem(yy, 2) * Y_ROWS
        return pl.ds(pl.multiple_of(row, UNIT), Y_ROWS)

    core_copies = []
    for o in (2, 1, 3, 0):
        yy = lax.rem(y + o, RING)
        core_copies.append(
            send(g_ref.at[piece(yy, 1 - core)], cbuf.at[o], core_s.at[o], core_r.at[o], dev_core)
        )
    own_loads = {}
    for o in (2, 1, 3, 0):
        own_loads[o] = pltpu.make_async_copy(
            g_ref.at[piece(lax.rem(y + o, RING), core)], gown.at[o], own_sem.at[o]
        )
        own_loads[o].start()
    half = Y_ROWS // 2
    lo, hi = pl.ds(0, half), pl.ds(half, half)

    def summed(o):
        return gown[o] + cbuf[o]

    for load in own_loads.values():
        load.wait()
    core_copies[0].wait_recv()
    ysend[1] = summed(2).astype(jnp.bfloat16)
    y0 = send(ysend.at[1, lo], yfirst.at[0], y_s.at[0], y_r.at[0], dev_yr)
    y1 = send(ysend.at[1, hi], yfirst.at[1], y_s.at[1], y_r.at[1], dev_yl)
    core_copies[1].wait_recv()
    ysend[0] = summed(1).astype(jnp.bfloat16)
    y2 = send(ysend.at[0, hi], yfrom.at[0, hi], y_s.at[2], y_r.at[2], dev_yr)
    core_copies[2].wait_recv()
    ysend[2] = summed(3).astype(jnp.bfloat16)
    y3 = send(ysend.at[2, lo], yfrom.at[1, lo], y_s.at[3], y_r.at[3], dev_yl)
    core_copies[3].wait_recv()
    y0.wait_recv()
    part = summed(1)
    ystage[0] = (part[:half] + yfirst[0].astype(jnp.float32)).astype(jnp.bfloat16)
    y4 = send(ystage.at[0], yfrom.at[0, lo], y_s.at[4], y_r.at[4], dev_yr)
    y1.wait_recv()
    part = summed(3)
    ystage[1] = (part[half:] + yfirst[1].astype(jnp.float32)).astype(jnp.bfloat16)
    y5 = send(ystage.at[1], yfrom.at[1, hi], y_s.at[5], y_r.at[5], dev_yl)
    for copy in (y2, y3, y4, y5):
        copy.wait_recv()
    xbuf[...] = (
        summed(0) + yfrom[0].astype(jnp.float32) + yfrom[1].astype(jnp.float32)
    ).reshape(RING, X_ROWS, LANES)

    xh = X_ROWS // 2
    xlo, xhi = pl.ds(0, xh), pl.ds(xh, xh)
    x0 = send(xbuf.at[x_op, xlo], xfirst.at[0], x_s.at[0], x_r.at[0], dev_xr)
    x1 = send(xbuf.at[x_op, xhi], xfirst.at[1], x_s.at[1], x_r.at[1], dev_xl)
    x2 = send(xbuf.at[x_r1, xhi], xfrom.at[0, xhi], x_s.at[2], x_r.at[2], dev_xr)
    x3 = send(xbuf.at[x_l1, xlo], xfrom.at[1, xlo], x_s.at[3], x_r.at[3], dev_xl)
    x0.wait_recv()
    xstage[0] = xbuf[x_r1, xlo] + xfirst[0]
    x4 = send(xstage.at[0], xfrom.at[0, xlo], x_s.at[4], x_r.at[4], dev_xr)
    x1.wait_recv()
    xstage[1] = xbuf[x_l1, xhi] + xfirst[1]
    x5 = send(xstage.at[1], xfrom.at[1, xhi], x_s.at[5], x_r.at[5], dev_xl)
    for copy in (x2, x3, x4, x5):
        copy.wait_recv()
    zbuf[...] = (xbuf[x] + xfrom[0] + xfrom[1]).reshape(Z_OWNERS, UNIT, LANES)

    def z_copy(o):
        to = lax.rem(z + o, Z_SIZE)
        return pltpu.make_async_remote_copy(
            src_ref=zbuf.at[lax.min(to, Z_OWNERS - 1)],
            dst_ref=zfrom.at[o - 1],
            send_sem=z_s.at[o - 1],
            recv_sem=z_r.at[o - 1],
            device_id=dev_z(o),
            device_id_type=MESH_ID,
        )

    def own_rows(zz):
        row = y_lo * Y_ROWS + x * X_ROWS + lax.min(zz, Z_OWNERS - 1) * UNIT
        return final.at[pl.ds(pl.multiple_of(row, UNIT), UNIT)]

    def za_copy(o, zz):
        return pltpu.make_async_remote_copy(
            src_ref=own_rows(zz),
            dst_ref=own_rows(zz),
            send_sem=za_s.at[o - 1],
            recv_sem=za_r.at[o - 1],
            device_id=dev_z(o),
            device_id_type=MESH_ID,
        )

    for o in range(1, Z_SIZE):
        @pl.when(lax.rem(z + o, Z_SIZE) < Z_OWNERS)
        def _():
            z_copy(o).start()

    @pl.when(z < Z_OWNERS)
    def _():
        total = zbuf[lax.min(z, Z_OWNERS - 1)]
        for o in range(1, Z_SIZE):
            z_copy(o).wait_recv()
            total = total + zfrom[o - 1]
        row = y_lo * Y_ROWS + x * X_ROWS + lax.min(z, Z_OWNERS - 1) * UNIT
        final[pl.ds(pl.multiple_of(row, UNIT), UNIT)] = total.astype(jnp.bfloat16)
        for o in range(1, Z_SIZE):
            za_copy(o, z).start()

    for o in range(1, Z_SIZE):
        source = lax.rem(z + Z_SIZE - o, Z_SIZE)
        @pl.when(source < Z_OWNERS)
        def _():
            za_copy(o, source).wait_recv()

    def rows(xx, start, size):
        row = y_lo * Y_ROWS + xx * X_ROWS + start
        return final.at[pl.ds(pl.multiple_of(row, UNIT), size)]

    cut = 7 * UNIT
    mine = rows(x, 0, X_ROWS)
    a0 = send(mine, mine, xa_s.at[0], xa_r.at[0], dev_xr)
    a1 = send(mine, mine, xa_s.at[1], xa_r.at[1], dev_xl)
    b0 = send(mine, mine, ya_s.at[0], ya_r.at[0], dev_mate)
    a0.wait_recv()
    ring_lo = rows(x_l1, 0, cut)
    a2 = send(ring_lo, ring_lo, xa_s.at[2], xa_r.at[2], dev_xr)
    got = rows(x_l1, 0, X_ROWS)
    b1 = send(got, got, ya_s.at[1], ya_r.at[1], dev_mate)
    a1.wait_recv()
    ring_hi = rows(x_r1, cut, X_ROWS - cut)
    a3 = send(ring_hi, ring_hi, xa_s.at[3], xa_r.at[3], dev_xl)
    got = rows(x_r1, 0, X_ROWS)
    b2 = send(got, got, ya_s.at[2], ya_r.at[2], dev_mate)
    a2.wait_recv()
    a3.wait_recv()
    got = rows(x_op, 0, X_ROWS)
    b3 = send(got, got, ya_s.at[3], ya_r.at[3], dev_mate)
    for copy in (b0, b1, b2, b3):
        copy.wait_recv()

    tile_rows = o_ref.shape[0]
    for i in range(o_ref.shape[1] // LANES):
        o_ref[:, i * LANES : (i + 1) * LANES] = final[
            i * tile_rows : (i + 1) * tile_rows
        ].astype(jnp.float32)

    for copy in core_copies + [y0, y1, y2, y3, y4, y5, x0, x1, x2, x3, x4, x5]:
        copy.wait_send()
    for o in range(1, Z_SIZE):
        @pl.when(lax.rem(z + o, Z_SIZE) < Z_OWNERS)
        def _():
            z_copy(o).wait_send()

    @pl.when(z < Z_OWNERS)
    def _():
        for o in range(1, Z_SIZE):
            za_copy(o, z).wait_send()
    for copy in (a0, a1, a2, a3, b0, b1, b2, b3):
        copy.wait_send()


def reduce_gradients(packed, rows, cols):
    f32, bf16 = jnp.float32, jnp.bfloat16
    half, xh = Y_ROWS // 2, X_ROWS // 2
    dma = pltpu.SemaphoreType.DMA
    return pl.pallas_call(
        reduce_kernel,
        out_shape=jax.ShapeDtypeStruct((rows, cols), f32),
        in_specs=[pl.BlockSpec(memory_space=pltpu.HBM)],
        out_specs=pl.BlockSpec(memory_space=pltpu.VMEM),
        scratch_shapes=[
            pltpu.VMEM((RING, Y_ROWS, LANES), f32),
            dma((RING,)),
            pltpu.VMEM((RING, Y_ROWS, LANES), f32),
            pltpu.VMEM((3, Y_ROWS, LANES), bf16),
            pltpu.VMEM((2, half, LANES), bf16),
            pltpu.VMEM((2, half, LANES), bf16),
            pltpu.VMEM((2, Y_ROWS, LANES), bf16),
            pltpu.VMEM((RING, X_ROWS, LANES), f32),
            pltpu.VMEM((2, xh, LANES), f32),
            pltpu.VMEM((2, xh, LANES), f32),
            pltpu.VMEM((2, X_ROWS, LANES), f32),
            pltpu.VMEM((Z_OWNERS, UNIT, LANES), f32),
            pltpu.VMEM((Z_SIZE - 1, UNIT, LANES), f32),
            pltpu.VMEM((Q_ROWS, LANES), bf16),
            dma((RING,)), dma((RING,)),
            dma((6,)), dma((6,)),
            dma((6,)), dma((6,)),
            dma((Z_SIZE - 1,)), dma((Z_SIZE - 1,)),
            dma((Z_SIZE - 1,)), dma((Z_SIZE - 1,)),
            dma((4,)), dma((4,)),
            dma((4,)), dma((4,)),
        ],
        compiler_params=pltpu.CompilerParams(
            collective_id=0, has_side_effects=True, vmem_limit_bytes=56 << 20
        ),
        name="reduce_gradients",
    )(packed)


def per_device(
    members, cached, send_rows, take_rows, utt_index, upstream, in_proj, norm_gain, conv_kernel
):
    moved = exchange(
        cached[0, 0], send_rows[0, 0], take_rows[0, 0], utt_index[0, 0], upstream[0, 0],
        in_proj, conv_kernel, norm_gain, members,
    )
    packed, device_loss = module_terms(*moved)
    depth, cols = in_proj.shape
    total = reduce_gradients(packed, depth + TAPS + 1, cols)
    return (
        total[:depth],
        total[depth : depth + TAPS],
        total[depth + TAPS],
        device_loss,
    )


def solution(mesh):
    placed = (
        P("dp", "fsdp", None, None),
        P("dp", "fsdp", None, None),
        P("dp", "fsdp", None),
        P("dp", "fsdp", None),
        P("dp", "fsdp", None, None),
        P(None, "fsdp"),
        P("fsdp"),
        P(None, "fsdp"),
    )
    return jax.shard_map(
        functools.partial(per_device, mesh.shape["fsdp"]),
        mesh=mesh,
        in_specs=placed,
        out_specs=(P(None, "fsdp"), P(None, "fsdp"), P("fsdp"), P("dp", "fsdp")),
        check_vma=False,
    )
```

```python
import functools

import jax
import jax.numpy as jnp
from jax import lax
from jax.experimental import pallas as pl
from jax.experimental.pallas import tpu as pltpu
from jax.sharding import PartitionSpec as P

LANES = 128
RING = 4
Z_SIZE = 16
UNIT = 16
Z_OWNERS = 13
X_ROWS = Z_OWNERS * UNIT
Y_ROWS = RING * X_ROWS
Q_ROWS = 2 * Y_ROWS
MESH_ID = pl.DeviceIdType.MESH


SUB = 8
SPAN = 42
HALO = 8
TAPS = 31
REACH = TAPS // 2
BLOCK = 14
GAP = 8
ROWS = SPAN * SUB


def module_kernel(fr_hbm, up_hbm, w_hbm, gain_hbm, taps_hbm, out_ref, loss_ref,
                  x_s, xh_s, go_s, h_s, inv_s, gc_s, sh_s, shx_s, gx_s, ft_s,
                  tb_s, cx_s, cg_s, p_s, q_s,
                  fr_ref, up_ref, w_ref, gain_ref, taps_ref, in_sem):
    f32, bf16 = jnp.float32, jnp.bfloat16
    loads = [
        pltpu.make_async_copy(src, dst, in_sem.at[i])
        for i, (src, dst) in enumerate(
            [
                (w_hbm, w_ref), (fr_hbm, fr_ref), (up_hbm, up_ref),
                (gain_hbm, gain_ref), (taps_hbm, taps_ref),
            ]
        )
    ]
    for load in loads:
        load.start()
    loads[0].wait()
    loads[1].wait()
    tiles = gain_ref.shape[0]
    width = tiles * LANES
    depth = w_ref.shape[0]
    scale = (2 * 256 * width) ** (-0.5)

    for h in range(2):
        frame = fr_ref[h * ROWS : (h + 1) * ROWS, :]
        ft_s[:, h * ROWS : (h + 1) * ROWS] = frame.T
        x_s[h] = jnp.dot(frame, w_ref[...], preferred_element_type=f32)

    for load in loads[2:]:
        load.wait()

    def norm_rows(i, loss):
        for h in range(2):
            at = pl.ds(pl.multiple_of(i * 16, 16), 16)
            xv = x_s[h, at, :]
            mean = jnp.sum(xv, axis=1, keepdims=True) * (1.0 / width)
            cen = xv - mean
            var = jnp.sum(cen * cen, axis=1, keepdims=True) * (1.0 / width)
            inv = lax.rsqrt(var + 1e-05)
            inv_s[h, pl.ds(2 * i, 2)] = jnp.broadcast_to(inv, (16, LANES)).reshape(2, SUB, LANES)
            for c in range(tiles):
                lanes = slice(c * LANES, (c + 1) * LANES)
                up = up_ref[pl.ds(pl.multiple_of(h * ROWS + i * 16, 16), 16), lanes]
                go = up.astype(f32) * scale
                go_s[c, h, pl.ds(2 * i, 2)] = go.reshape(2, SUB, LANES)
                xh_s[c, h, pl.ds(HALO + 2 * i, 2)] = (cen[:, lanes] * inv).reshape(2, SUB, LANES)
                loss = loss + go * xv[:, lanes]
        return loss

    loss = lax.fori_loop(0, SPAN // 2, norm_rows, jnp.zeros((16, LANES), f32))
    loss = loss[:SUB] + loss[SUB:]

    sub = lax.broadcasted_iota(jnp.int32, (SUB, LANES), 0)

    def fill_halo(ref):
        for h in range(2):
            for j in range(HALO):
                before = pltpu.roll(ref[h, SPAN + j], 1, 0)
                ref[h, j] = jnp.where(sub == 0, 0.0, before)
                after = pltpu.roll(ref[h, HALO + j], SUB - 1, 0)
                ref[h, HALO + SPAN + j] = jnp.where(sub == SUB - 1, 0.0, after)

    evens = range(-(REACH // 2), REACH // 2 + 1)
    odds = range(-(REACH // 2) - 1, REACH // 2 + 1)

    def even_tap(m):
        return 2 * m + REACH

    def odd_tap(m):
        return 2 * m + 1 + REACH

    def slide(get, taps, j0):
        accs = {}
        for i in range(min(taps), BLOCK + max(taps)):
            v = get(j0 + (HALO + i))
            for j in range(BLOCK):
                if i - j in taps:
                    term = taps[i - j] * v
                    accs[j] = accs[j] + term if j in accs else term
        return accs

    def cross_sums(ref, cross):
        for j in range(2 * HALO + SPAN - 1):
            cross[j] = ref[1, j] + ref[0, j + 1]

    def conv(ref, cross, tap, use, carry):
        def parts(b, c):
            j0 = b * BLOCK
            own = slide(lambda j: ref[0, j], {m: tap(even_tap(m)) for m in evens}, j0)
            for j, v in own.items():
                p_s[j0 + j] = v
            own = slide(lambda j: ref[1, j], {m: tap(odd_tap(m)) for m in odds}, j0)
            for j, v in own.items():
                q_s[j0 + j] = v
            return c

        lax.fori_loop(0, SPAN // BLOCK, parts, 0)
        cross_sums(ref, cross)
        p_s[SPAN] = jnp.where(sub == SUB - 1, 0.0, pltpu.roll(p_s[0], SUB - 1, 0))

        def joined(b, carry):
            j0 = b * BLOCK
            both = {}
            for m in odds:
                both[m] = tap(odd_tap(m)) + tap(even_tap(m)) if m in evens else tap(odd_tap(m))
            third = slide(lambda j: cross[j], both, j0)
            for j in range(BLOCK):
                q = q_s[j0 + j]
                carry = use(0, j0 + j, p_s[j0 + j] + q, carry)
                carry = use(1, j0 + j, third[j] - (p_s[j0 + (j + 1)] + q), carry)
            return carry

        return lax.fori_loop(0, SPAN // BLOCK, joined, carry)

    sh_s[...] = jnp.zeros_like(sh_s)
    shx_s[...] = jnp.zeros_like(shx_s)

    def channel_tile(ct, loss):
        xh = xh_s.at[ct]
        fill_halo(xh)
        gain = jnp.broadcast_to(gain_ref[ct], (SUB, LANES))
        for k in range(TAPS):
            tap = jnp.broadcast_to(taps_ref[ct, k : k + 1, :], (SUB, LANES))
            tb_s[0, k] = tap * gain
            tb_s[1, TAPS - 1 - k] = tap

        def forward(h, j, c, loss):
            sig = 1.0 / (1.0 + jnp.exp(-c))
            gos = go_s[ct, h, j] * sig
            gc_s[h, j + HALO] = gos * (1.0 + c * (1.0 - sig))
            return loss + c * gos

        loss = conv(xh, cx_s, lambda k: tb_s[0, k], forward, loss)
        fill_halo(gc_s)

        def backward(h, j, gn, gg):
            v = xh[h, j + HALO]
            hv = gn * gain
            h_s[ct, h, j] = hv
            sh_s[h, j] = sh_s[h, j] + hv
            shx_s[h, j] = shx_s[h, j] + hv * v
            return gg + gn * v

        zero = jnp.zeros((SUB, LANES), f32)
        gg = conv(gc_s, cg_s, lambda k: tb_s[1, k], backward, zero)

        def correlate(grad, get, offsets):
            def block(b, sums):
                j0 = b * BLOCK
                sums = dict(zip(offsets, sums))
                grads = [grad(j0 + (HALO + j)) for j in range(BLOCK)]
                for i in range(offsets[0], BLOCK + offsets[-1]):
                    v = get(j0 + (HALO + i))
                    for j in range(BLOCK):
                        if i - j in sums:
                            sums[i - j] = sums[i - j] + grads[j] * v
                return tuple(sums[m] for m in offsets)

            sums = lax.fori_loop(0, SPAN // BLOCK, block, (zero,) * len(offsets))
            return dict(zip(offsets, sums))

        even = correlate(lambda j: gc_s[0, j] - gc_s[1, j - 1], lambda j: xh[0, j], evens)
        for m in evens:
            tb_s[0, even_tap(m)] = even[m]
        odd = correlate(lambda j: gc_s[0, j] - gc_s[1, j], lambda j: xh[1, j], odds)
        for m in odds:
            tb_s[0, odd_tap(m)] = odd[m]
        both = correlate(lambda j: gc_s[1, j], lambda j: cx_s[j], odds)
        for m in odds:
            tb_s[0, odd_tap(m)] = tb_s[0, odd_tap(m)] + both[m]
            if m in evens:
                tb_s[0, even_tap(m)] = tb_s[0, even_tap(m)] + both[m]
        base = lax.div(ct, 3) * Q_ROWS + lax.rem(ct, 3) * (depth + TAPS + 1) + depth
        gain_row = gain_ref[ct]
        tail = [jnp.sum(tb_s[0, k], axis=0, keepdims=True) * gain_row for k in range(TAPS)]
        tail.append(jnp.sum(gg, axis=0, keepdims=True))
        out_ref[pl.ds(pl.multiple_of(base, SUB), TAPS + 1), :] = jnp.concatenate(tail, axis=0)
        return loss

    loss = lax.fori_loop(0, tiles, channel_tile, loss)
    loss_ref[...] = jnp.sum(loss, keepdims=True)

    def grad_rows(i, carry):
        for h in range(2):
            two = pl.ds(2 * i, 2)
            mh = jnp.sum(sh_s[h, two], axis=2, keepdims=True) * (1.0 / width)
            mhx = jnp.sum(shx_s[h, two], axis=2, keepdims=True) * (1.0 / width)
            inv = inv_s[h, two]
            for c in range(tiles):
                xv = xh_s[c, h, pl.ds(HALO + 2 * i, 2)]
                gx = go_s[c, h, two] + inv * (h_s[c, h, two] - mh - xv * mhx)
                gx_s[pl.ds(pl.multiple_of(h * ROWS + i * 16, 16), 16), c * LANES : (c + 1) * LANES] = (
                    gx.reshape(16, LANES).astype(bf16)
                )
        return carry

    lax.fori_loop(0, SPAN // 2, grad_rows, 0)

    per = 2 * LANES
    for c in range(0, tiles, 2):
        gw = jnp.dot(ft_s[...], gx_s[:, c * LANES : c * LANES + per], preferred_element_type=f32)
        for k in range(2):
            base = (c + k) // 3 * Q_ROWS + (c + k) % 3 * (depth + TAPS + 1)
            out_ref[base : base + depth, :] = gw[:, k * LANES : (k + 1) * LANES]
    used = 3 * (depth + TAPS + 1)
    for q in range(tiles // 3):
        out_ref[q * Q_ROWS + used : (q + 1) * Q_ROWS, :] = jnp.zeros((Q_ROWS - used, LANES), f32)


def module_terms(frames, above, proj, tap_tiles, gain_tiles):
    f32, bf16 = jnp.float32, jnp.bfloat16
    tiles = proj.shape[1] // LANES
    depth = proj.shape[0]
    vm = pl.BlockSpec(memory_space=pltpu.VMEM)
    rows = (2, SPAN, SUB, LANES)
    return pl.pallas_call(
        module_kernel,
        out_shape=(
            jax.ShapeDtypeStruct((tiles // 3 * Q_ROWS, LANES), f32),
            jax.ShapeDtypeStruct((1, 1), f32),
        ),
        in_specs=[pl.BlockSpec(memory_space=pltpu.HBM)] * 5,
        out_specs=(vm, vm),
        scratch_shapes=[
            pltpu.VMEM((2, ROWS, tiles * LANES), f32),
            pltpu.VMEM((tiles, 2, SPAN + 2 * HALO, SUB, LANES), f32),
            pltpu.VMEM((tiles,) + rows, f32),
            pltpu.VMEM((tiles,) + rows, f32),
            pltpu.VMEM(rows, f32),
            pltpu.VMEM((2, SPAN + 2 * HALO, SUB, LANES), f32),
            pltpu.VMEM(rows, f32),
            pltpu.VMEM(rows, f32),
            pltpu.VMEM((2 * ROWS, tiles * LANES), bf16),
            pltpu.VMEM((depth, 2 * ROWS), bf16),
            pltpu.VMEM((2, TAPS, SUB, LANES), f32),
            pltpu.VMEM((SPAN + 2 * HALO, SUB, LANES), f32),
            pltpu.VMEM((SPAN + 2 * HALO, SUB, LANES), f32),
            pltpu.VMEM((SPAN + 1, SUB, LANES), f32),
            pltpu.VMEM((SPAN, SUB, LANES), f32),
            pltpu.VMEM(frames.shape, bf16),
            pltpu.VMEM(above.shape, bf16),
            pltpu.VMEM(proj.shape, bf16),
            pltpu.VMEM(gain_tiles.shape, f32),
            pltpu.VMEM(tap_tiles.shape, f32),
            pltpu.SemaphoreType.DMA((5,)),
        ],
        compiler_params=pltpu.CompilerParams(vmem_limit_bytes=56 << 20),
        name="module_terms",
    )(frames, above, proj, gain_tiles, tap_tiles)


def exchange_kernel(
    cache_hbm, want_hbm, take_hbm, utt_hbm, up_hbm, w_ref, taps_ref, gain_ref,
    fr_ref, above_hbm, proj_hbm, tapt_ref, gaint_ref,
    above_ref, proj_ref, pick_s, send_s, arr_s, taps_s, gain_s,
    cache_ref, want_ref, take_ref, utt_ref, up_ref,
    row_s, row_r, par_s, par_r, in_sem, out_sem,
):
    f32, bf16 = jnp.float32, jnp.bfloat16
    peers = arr_s.shape[0]
    members = proj_ref.shape[1] // w_ref.shape[1]
    cols = w_ref.shape[1]
    p = lax.axis_index("dp")
    f = lax.axis_index("fsdp")

    def peer(o):
        return lax.rem(p + o, peers)

    own = pl.ds(pl.multiple_of(f * cols, LANES), cols)
    loads = [
        pltpu.make_async_copy(src, dst, in_sem.at[i])
        for i, (src, dst) in enumerate(
            [
                (want_hbm, want_ref), (cache_hbm, cache_ref), (take_hbm, take_ref),
                (utt_hbm, utt_ref), (up_hbm, up_ref), (w_ref, proj_ref.at[:, own]),
                (taps_ref, taps_s.at[:, own]), (gain_ref, gain_s.at[:, own]),
            ]
        )
    ]
    for load in loads:
        load.start()

    barrier = pltpu.get_barrier_semaphore()

    def greet(o, carry):
        pl.semaphore_signal(barrier, inc=1, device_id=(peer(o), f), device_id_type=MESH_ID)
        return carry

    lax.fori_loop(1, peers, greet, 0)
    for o in range(1, members):
        pl.semaphore_signal(
            barrier, inc=1, device_id=(p, lax.rem(f + o, members)), device_id_type=MESH_ID
        )

    count, width = cache_ref.shape
    half = width // 2
    loads[0].wait()
    loads[1].wait()
    want = jnp.concatenate([want_ref[...], want_ref[...]], axis=0)
    cache_ids = lax.broadcasted_iota(jnp.int32, (SUB, count), 1)
    for d in range(0, peers, 2):
        two = [
            (jnp.broadcast_to(want[:, d + k : d + k + 1], (SUB, count)) == cache_ids).astype(f32)
            for k in range(2)
        ]
        pick_s[d * SUB : (d + 2) * SUB, :count] = jnp.concatenate(two, axis=0).astype(bf16)
    step = 256
    first = lax.broadcasted_iota(jnp.int32, (step, half), 0) % SUB < SUB // 2
    for r in range(0, peers * SUB, step):
        rows = jnp.dot(pick_s[r : r + step, :count], cache_ref[...], preferred_element_type=f32)
        rows = jnp.where(first, rows[:, :half], rows[:, half:])
        send_s[r // SUB : (r + step) // SUB] = rows.reshape(step // SUB, SUB, half).astype(bf16)

    pl.semaphore_wait(barrier, peers - 1 + members - 1)

    def row_copy(o):
        return pltpu.make_async_remote_copy(
            src_ref=send_s.at[peer(o)],
            dst_ref=arr_s.at[p],
            send_sem=row_s,
            recv_sem=row_r,
            device_id=(peer(o), f),
            device_id_type=MESH_ID,
        )

    def param_copies(o):
        lanes = pl.ds(pl.multiple_of(f * cols, LANES), cols)
        pairs = [(w_ref, proj_ref), (taps_ref, taps_s), (gain_ref, gain_s)]
        return [
            pltpu.make_async_remote_copy(
                src_ref=src,
                dst_ref=dst.at[:, lanes],
                send_sem=par_s.at[3 * (o - 1) + i],
                recv_sem=par_r.at[3 * (o - 1) + i],
                device_id=(p, lax.rem(f + o, members)),
                device_id_type=MESH_ID,
            )
            for i, (src, dst) in enumerate(pairs)
        ]

    row_copy(peers // 2).start()

    def start_rows(i, carry):
        o = peers // 2 - i
        row_copy(o).start()
        row_copy(peers - o).start()
        return carry

    lax.fori_loop(1, peers // 2, start_rows, 0)
    for o in range(1, members):
        for copy in param_copies(o):
            copy.start()
    arr_s[p] = send_s[p]
    for load in loads[2:]:
        load.wait()

    sub = lax.broadcasted_iota(jnp.int32, (SUB, 1), 0)
    steps = up_ref.shape[0]
    slots = take_ref.shape[1]
    place = lax.broadcasted_iota(jnp.int32, (1, slots), 1) + GAP * utt_ref[...]
    place = jnp.broadcast_to(jnp.where(take_ref[...] >= 0, place, -1), (SUB, slots))
    take = jnp.broadcast_to(take_ref[...], (SUB, slots))
    for j in range(0, SPAN, 2):
        two = [(place == sub * SPAN + (j + k)).astype(f32) for k in range(2)]
        pick_s[j * SUB : (j + 2) * SUB, steps : steps + slots] = (
            jnp.concatenate(two, axis=0).astype(bf16)
        )
    slot_ids = lax.broadcasted_iota(jnp.int32, (slots, steps), 0)
    step_ids = lax.broadcasted_iota(jnp.int32, (slots, steps), 1)
    for h in range(2):
        spread = (step_ids == 2 * slot_ids + h).astype(f32).astype(bf16)
        pick_s[h * ROWS : (h + 1) * ROWS, :steps] = jnp.dot(
            pick_s[:ROWS, steps : steps + slots], spread, preferred_element_type=f32
        ).astype(bf16)
    for r in range(0, 2 * ROWS, ROWS // 2):
        above_ref[r : r + ROWS // 2, :] = jnp.dot(
            pick_s[r : r + ROWS // 2, :steps], up_ref[...], preferred_element_type=f32
        ).astype(bf16)
    arrived = lax.broadcasted_iota(jnp.int32, (SUB, peers * SUB), 1)
    for j in range(0, SPAN, 2):
        twos = ([], [])
        for k in range(2):
            held = place == sub * SPAN + (j + k)
            taken = jnp.max(jnp.where(held, take, -1), axis=1, keepdims=True)
            taken = jnp.where(taken < 0, -SUB, taken + taken // 4 * 4)
            for h in range(2):
                twos[h].append((jnp.broadcast_to(taken + 4 * h, arrived.shape) == arrived).astype(f32))
        for h in range(2):
            row = h * ROWS + j * SUB
            pick_s[row : row + 2 * SUB, :] = jnp.concatenate(twos[h], axis=0).astype(bf16)

    for o in range(1, members):
        for copy in param_copies(o):
            copy.wait_recv()
    leaving = [
        pltpu.make_async_copy(above_ref, above_hbm, out_sem.at[0]),
        pltpu.make_async_copy(proj_ref, proj_hbm, out_sem.at[1]),
    ]
    for copy in leaving:
        copy.start()
    tiles = gaint_ref.shape[0]
    for c in range(tiles):
        lanes = slice(c * LANES, (c + 1) * LANES)
        tapt_ref[c] = taps_s[:, lanes].astype(f32)
        gaint_ref[c] = gain_s[:, lanes].astype(f32)

    whole = pltpu.make_async_remote_copy(
        src_ref=send_s.at[pl.ds(0, peers - 1)],
        dst_ref=arr_s.at[pl.ds(0, peers - 1)],
        send_sem=row_s,
        recv_sem=row_r,
        device_id=(peer(1), f),
        device_id_type=MESH_ID,
    )
    whole.wait_recv()
    table = arr_s[...].astype(f32).reshape(peers * SUB, half).astype(bf16)
    for h in range(2):
        rows = slice(h * ROWS, (h + 1) * ROWS)
        fr_ref[rows, :] = jnp.dot(pick_s[rows, :], table, preferred_element_type=f32).astype(bf16)
    whole.wait_send()
    for o in range(1, members):
        for copy in param_copies(o):
            copy.wait_send()
    for copy in leaving:
        copy.wait()


def exchange(cache_rows, wanted, take, utt, upstream, in_proj, taps, gain, members):
    f32, bf16, i32 = jnp.float32, jnp.bfloat16, jnp.int32
    peers = wanted.shape[0]
    slots = take.shape[0]
    depth, cols = in_proj.shape
    width = cols * members
    tiles = width // LANES
    half = cache_rows.shape[1] // 2
    vm = pl.BlockSpec(memory_space=pltpu.VMEM)
    dma = pltpu.SemaphoreType.DMA
    shape = jax.ShapeDtypeStruct
    return pl.pallas_call(
        exchange_kernel,
        out_shape=(
            shape((2 * ROWS, half), bf16),
            shape((2 * ROWS, width), bf16),
            shape((depth, width), bf16),
            shape((tiles, TAPS, LANES), f32),
            shape((tiles, 1, LANES), f32),
        ),
        in_specs=[pl.BlockSpec(memory_space=pltpu.HBM)] * 8,
        out_specs=(
            vm,
            pl.BlockSpec(memory_space=pltpu.HBM),
            pl.BlockSpec(memory_space=pltpu.HBM),
            vm,
            vm,
        ),
        scratch_shapes=[
            pltpu.VMEM((2 * ROWS, width), bf16),
            pltpu.VMEM((depth, width), bf16),
            pltpu.VMEM((max(2 * ROWS, peers * SUB), peers * SUB), bf16),
            pltpu.VMEM((peers, SUB, half), bf16),
            pltpu.VMEM((peers, SUB, half), bf16),
            pltpu.VMEM((TAPS, width), bf16),
            pltpu.VMEM((1, width), bf16),
            pltpu.VMEM(cache_rows.shape, bf16),
            pltpu.VMEM(wanted.shape[::-1], i32),
            pltpu.VMEM((1, slots), i32),
            pltpu.VMEM((1, slots), i32),
            pltpu.VMEM(upstream.shape, bf16),
            dma, dma,
            dma((3 * (members - 1),)), dma((3 * (members - 1),)),
            dma((8,)),
            dma((2,)),
        ],
        compiler_params=pltpu.CompilerParams(
            collective_id=1, has_side_effects=True, vmem_limit_bytes=56 << 20
        ),
        name="exchange",
    )(
        cache_rows, wanted.T, take[None, :], utt[None, :], upstream,
        in_proj, taps, gain[None, :],
    )


def reduce_kernel(
    g_ref, proj_ref, taps_ref, gain_ref,
    gown, own_sem, cbuf, ysend, ystage, yfirst, yfrom,
    xbuf, xstage, xfirst, xfrom,
    zbuf, zfrom, final,
    core_s, core_r, y_s, y_r, x_s, x_r, z_s, z_r, za_s, za_r, xa_s, xa_r, ya_s, ya_r,
):
    p = lax.axis_index("dp")
    f = lax.axis_index("fsdp")
    x = lax.rem(p, RING)
    z = lax.rem(lax.div(p, RING), Z_SIZE)
    y_lo = lax.div(p, RING * Z_SIZE)
    y_hi = lax.div(f, 2)
    core = lax.rem(f, 2)
    y = y_hi * 2 + y_lo

    def at(yy, zz, xx, cc):
        return (
            (lax.rem(yy, 2) * Z_SIZE + zz) * RING + xx,
            lax.div(yy, 2) * 2 + cc,
        )

    y_r1, y_l1, y_op = lax.rem(y + 1, RING), lax.rem(y + 3, RING), lax.rem(y + 2, RING)
    x_r1, x_l1, x_op = lax.rem(x + 1, RING), lax.rem(x + 3, RING), lax.rem(x + 2, RING)
    y_mate = y_hi * 2 + 1 - y_lo
    dev_core = at(y, z, x, 1 - core)
    dev_yr, dev_yl = at(y_r1, z, x, core), at(y_l1, z, x, core)
    dev_xr, dev_xl = at(y, z, x_r1, core), at(y, z, x_l1, core)
    dev_mate = at(y_mate, z, x, core)

    def dev_z(o):
        return at(y, lax.rem(z + o, Z_SIZE), x, core)

    barrier = pltpu.get_barrier_semaphore()
    for d in [dev_core, dev_yr, dev_yl, dev_xr, dev_xl]:
        pl.semaphore_signal(barrier, inc=1, device_id=d, device_id_type=MESH_ID)
    for o in range(1, Z_SIZE):
        pl.semaphore_signal(barrier, inc=1, device_id=dev_z(o), device_id_type=MESH_ID)
    pl.semaphore_wait(barrier, 5 + Z_SIZE - 1)

    def send(src, dst, ssem, rsem, d):
        copy = pltpu.make_async_remote_copy(
            src_ref=src, dst_ref=dst, send_sem=ssem, recv_sem=rsem,
            device_id=d, device_id_type=MESH_ID,
        )
        copy.start()
        return copy

    def piece(yy, cc):
        row = (lax.div(yy, 2) * 2 + cc) * Q_ROWS + lax.rem(yy, 2) * Y_ROWS
        return pl.ds(pl.multiple_of(row, UNIT), Y_ROWS)

    core_copies = []
    for o in (2, 1, 3, 0):
        yy = lax.rem(y + o, RING)
        core_copies.append(
            send(g_ref.at[piece(yy, 1 - core)], cbuf.at[o], core_s.at[o], core_r.at[o], dev_core)
        )
    own_loads = {}
    for o in (2, 1, 3, 0):
        own_loads[o] = pltpu.make_async_copy(
            g_ref.at[piece(lax.rem(y + o, RING), core)], gown.at[o], own_sem.at[o]
        )
        own_loads[o].start()
    half = Y_ROWS // 2
    lo, hi = pl.ds(0, half), pl.ds(half, half)

    def summed(o):
        return gown[o] + cbuf[o]

    for load in own_loads.values():
        load.wait()
    core_copies[0].wait_recv()
    ysend[1] = summed(2).astype(jnp.bfloat16)
    y0 = send(ysend.at[1, lo], yfirst.at[0], y_s.at[0], y_r.at[0], dev_yr)
    y1 = send(ysend.at[1, hi], yfirst.at[1], y_s.at[1], y_r.at[1], dev_yl)
    core_copies[1].wait_recv()
    ysend[0] = summed(1).astype(jnp.bfloat16)
    y2 = send(ysend.at[0, hi], yfrom.at[0, hi], y_s.at[2], y_r.at[2], dev_yr)
    core_copies[2].wait_recv()
    ysend[2] = summed(3).astype(jnp.bfloat16)
    y3 = send(ysend.at[2, lo], yfrom.at[1, lo], y_s.at[3], y_r.at[3], dev_yl)
    core_copies[3].wait_recv()
    y0.wait_recv()
    part = summed(1)
    ystage[0] = (part[:half] + yfirst[0].astype(jnp.float32)).astype(jnp.bfloat16)
    y4 = send(ystage.at[0], yfrom.at[0, lo], y_s.at[4], y_r.at[4], dev_yr)
    y1.wait_recv()
    part = summed(3)
    ystage[1] = (part[half:] + yfirst[1].astype(jnp.float32)).astype(jnp.bfloat16)
    y5 = send(ystage.at[1], yfrom.at[1, hi], y_s.at[5], y_r.at[5], dev_yl)
    for copy in (y2, y3, y4, y5):
        copy.wait_recv()
    xbuf[...] = (
        summed(0) + yfrom[0].astype(jnp.float32) + yfrom[1].astype(jnp.float32)
    ).reshape(RING, X_ROWS, LANES)

    xh = X_ROWS // 2
    xlo, xhi = pl.ds(0, xh), pl.ds(xh, xh)
    x0 = send(xbuf.at[x_op, xlo], xfirst.at[0], x_s.at[0], x_r.at[0], dev_xr)
    x1 = send(xbuf.at[x_op, xhi], xfirst.at[1], x_s.at[1], x_r.at[1], dev_xl)
    x2 = send(xbuf.at[x_r1, xhi], xfrom.at[0, xhi], x_s.at[2], x_r.at[2], dev_xr)
    x3 = send(xbuf.at[x_l1, xlo], xfrom.at[1, xlo], x_s.at[3], x_r.at[3], dev_xl)
    x0.wait_recv()
    xstage[0] = xbuf[x_r1, xlo] + xfirst[0]
    x4 = send(xstage.at[0], xfrom.at[0, xlo], x_s.at[4], x_r.at[4], dev_xr)
    x1.wait_recv()
    xstage[1] = xbuf[x_l1, xhi] + xfirst[1]
    x5 = send(xstage.at[1], xfrom.at[1, xhi], x_s.at[5], x_r.at[5], dev_xl)
    for copy in (x2, x3, x4, x5):
        copy.wait_recv()
    zbuf[...] = (xbuf[x] + xfrom[0] + xfrom[1]).reshape(Z_OWNERS, UNIT, LANES)

    def z_copy(o):
        to = lax.rem(z + o, Z_SIZE)
        return pltpu.make_async_remote_copy(
            src_ref=zbuf.at[lax.min(to, Z_OWNERS - 1)],
            dst_ref=zfrom.at[o - 1],
            send_sem=z_s.at[o - 1],
            recv_sem=z_r.at[o - 1],
            device_id=dev_z(o),
            device_id_type=MESH_ID,
        )

    def own_rows(zz):
        row = y_lo * Y_ROWS + x * X_ROWS + lax.min(zz, Z_OWNERS - 1) * UNIT
        return final.at[pl.ds(pl.multiple_of(row, UNIT), UNIT)]

    def za_copy(o, zz):
        return pltpu.make_async_remote_copy(
            src_ref=own_rows(zz),
            dst_ref=own_rows(zz),
            send_sem=za_s.at[o - 1],
            recv_sem=za_r.at[o - 1],
            device_id=dev_z(o),
            device_id_type=MESH_ID,
        )

    for o in range(1, Z_SIZE):
        @pl.when(lax.rem(z + o, Z_SIZE) < Z_OWNERS)
        def _():
            z_copy(o).start()

    @pl.when(z < Z_OWNERS)
    def _():
        total = zbuf[lax.min(z, Z_OWNERS - 1)]
        for o in range(1, Z_SIZE):
            z_copy(o).wait_recv()
            total = total + zfrom[o - 1]
        row = y_lo * Y_ROWS + x * X_ROWS + lax.min(z, Z_OWNERS - 1) * UNIT
        final[pl.ds(pl.multiple_of(row, UNIT), UNIT)] = total.astype(jnp.bfloat16)
        for o in range(1, Z_SIZE):
            za_copy(o, z).start()

    for o in range(1, Z_SIZE):
        source = lax.rem(z + Z_SIZE - o, Z_SIZE)
        @pl.when(source < Z_OWNERS)
        def _():
            za_copy(o, source).wait_recv()

    def rows(xx, start, size):
        row = y_lo * Y_ROWS + xx * X_ROWS + start
        return final.at[pl.ds(pl.multiple_of(row, UNIT), size)]

    cut = 7 * UNIT
    mine = rows(x, 0, X_ROWS)
    a0 = send(mine, mine, xa_s.at[0], xa_r.at[0], dev_xr)
    a1 = send(mine, mine, xa_s.at[1], xa_r.at[1], dev_xl)
    b0 = send(mine, mine, ya_s.at[0], ya_r.at[0], dev_mate)
    a0.wait_recv()
    ring_lo = rows(x_l1, 0, cut)
    a2 = send(ring_lo, ring_lo, xa_s.at[2], xa_r.at[2], dev_xr)
    got = rows(x_l1, 0, X_ROWS)
    b1 = send(got, got, ya_s.at[1], ya_r.at[1], dev_mate)
    a1.wait_recv()
    ring_hi = rows(x_r1, cut, X_ROWS - cut)
    a3 = send(ring_hi, ring_hi, xa_s.at[3], xa_r.at[3], dev_xl)
    got = rows(x_r1, 0, X_ROWS)
    b2 = send(got, got, ya_s.at[2], ya_r.at[2], dev_mate)
    a2.wait_recv()
    a3.wait_recv()
    got = rows(x_op, 0, X_ROWS)
    b3 = send(got, got, ya_s.at[3], ya_r.at[3], dev_mate)
    for copy in (b0, b1, b2, b3):
        copy.wait_recv()

    depth, cols = proj_ref.shape
    tile_rows = depth + TAPS + 1
    for i in range(cols // LANES):
        lanes = slice(i * LANES, (i + 1) * LANES)
        top = i * tile_rows
        proj_ref[:, lanes] = final[top : top + depth].astype(jnp.float32)
        tail = final[top + depth : top + tile_rows].astype(jnp.float32)
        taps_ref[:, lanes] = tail[:TAPS]
        gain_ref[:, lanes] = tail[TAPS:]

    for copy in core_copies + [y0, y1, y2, y3, y4, y5, x0, x1, x2, x3, x4, x5]:
        copy.wait_send()
    for o in range(1, Z_SIZE):
        @pl.when(lax.rem(z + o, Z_SIZE) < Z_OWNERS)
        def _():
            z_copy(o).wait_send()

    @pl.when(z < Z_OWNERS)
    def _():
        for o in range(1, Z_SIZE):
            za_copy(o, z).wait_send()
    for copy in (a0, a1, a2, a3, b0, b1, b2, b3):
        copy.wait_send()


def reduce_gradients(packed, rows, cols):
    f32, bf16 = jnp.float32, jnp.bfloat16
    half, xh = Y_ROWS // 2, X_ROWS // 2
    dma = pltpu.SemaphoreType.DMA
    return pl.pallas_call(
        reduce_kernel,
        out_shape=tuple(
            jax.ShapeDtypeStruct((size, cols), f32) for size in (rows - TAPS - 1, TAPS, 1)
        ),
        in_specs=[pl.BlockSpec(memory_space=pltpu.HBM)],
        out_specs=(pl.BlockSpec(memory_space=pltpu.VMEM),) * 3,
        scratch_shapes=[
            pltpu.VMEM((RING, Y_ROWS, LANES), f32),
            dma((RING,)),
            pltpu.VMEM((RING, Y_ROWS, LANES), f32),
            pltpu.VMEM((3, Y_ROWS, LANES), bf16),
            pltpu.VMEM((2, half, LANES), bf16),
            pltpu.VMEM((2, half, LANES), bf16),
            pltpu.VMEM((2, Y_ROWS, LANES), bf16),
            pltpu.VMEM((RING, X_ROWS, LANES), f32),
            pltpu.VMEM((2, xh, LANES), f32),
            pltpu.VMEM((2, xh, LANES), f32),
            pltpu.VMEM((2, X_ROWS, LANES), f32),
            pltpu.VMEM((Z_OWNERS, UNIT, LANES), f32),
            pltpu.VMEM((Z_SIZE - 1, UNIT, LANES), f32),
            pltpu.VMEM((Q_ROWS, LANES), bf16),
            dma((RING,)), dma((RING,)),
            dma((6,)), dma((6,)),
            dma((6,)), dma((6,)),
            dma((Z_SIZE - 1,)), dma((Z_SIZE - 1,)),
            dma((Z_SIZE - 1,)), dma((Z_SIZE - 1,)),
            dma((4,)), dma((4,)),
            dma((4,)), dma((4,)),
        ],
        compiler_params=pltpu.CompilerParams(
            collective_id=0, has_side_effects=True, vmem_limit_bytes=61 << 20
        ),
        name="reduce_gradients",
    )(packed)


def per_device(
    members, cached, send_rows, take_rows, utt_index, upstream, in_proj, norm_gain, conv_kernel
):
    moved = exchange(
        cached[0, 0], send_rows[0, 0], take_rows[0, 0], utt_index[0, 0], upstream[0, 0],
        in_proj, conv_kernel, norm_gain, members,
    )
    packed, device_loss = module_terms(*moved)
    depth, cols = in_proj.shape
    grad_proj, grad_taps, grad_gain = reduce_gradients(packed, depth + TAPS + 1, cols)
    return (grad_proj, grad_taps, grad_gain[0], device_loss)


def solution(mesh):
    placed = (
        P("dp", "fsdp", None, None),
        P("dp", "fsdp", None, None),
        P("dp", "fsdp", None),
        P("dp", "fsdp", None),
        P("dp", "fsdp", None, None),
        P(None, "fsdp"),
        P("fsdp"),
        P(None, "fsdp"),
    )
    return jax.shard_map(
        functools.partial(per_device, mesh.shape["fsdp"]),
        mesh=mesh,
        in_specs=placed,
        out_specs=(P(None, "fsdp"), P(None, "fsdp"), P("fsdp"), P("dp", "fsdp")),
        check_vma=False,
    )
```
